32 devices in a mesh: groups: 2 (over y), ctx: 4 (over z), kv: 2 (over x), khalf: 2 (over core).
Axes of the slice: x: 2, y: 2, z: 4, core: 2. Of those that a mesh axis runs over, the one named last changes fastest.
Arguments:
- queries: bfloat16 [256, 8192], P(('groups', 'ctx'), 'kv'), parts along dimension 0, may hold values from -100 to 100
- cache_keys: bfloat16 [49152, 1024], P(('groups', 'ctx', 'khalf'), 'kv'), parts along dimension 0, may hold values from -7 to 7
- cache_values: bfloat16 [49152, 1024], P(('groups', 'ctx', 'khalf'), 'kv'), parts along dimension 0, may hold values from -6 to 6
- new_keys: bfloat16 [256, 1024], P(('groups', 'ctx'), 'kv'), parts along dimension 0, may hold values from -10 to 10
- new_values: bfloat16 [256, 1024], P(('groups', 'ctx'), 'kv'), parts along dimension 0, may hold values from -6 to 6
- cache_blocks: int32 [2], P('groups'), parts along dimension 0, may hold values from 48 to 192
- residual: bfloat16 [256, 8192], P('groups', ('ctx', 'khalf')), parts along dimension 0, may hold values from -20 to 20
- norm_gain: float32 [8192], P(('ctx', 'khalf')), may hold values from 0.1 to 1.9
- out_weight: bfloat16 [8192, 8192], P('kv', ('ctx', 'khalf')), may hold values from -0.0625 to 0.0625
- gate_up: bfloat16 [8192, 2, 14336], P(('ctx', 'khalf'), None, 'kv'), may hold values from -0.0625 to 0.0625
- down_weight: bfloat16 [14336, 8192], P('kv', ('ctx', 'khalf')), may hold values from -0.046875 to 0.046875
Outputs:
- layer_out: bfloat16 [256, 8192], P(('groups', 'kv'), ('ctx', 'khalf')), parts along dimension 0
The draws below stay inside these ranges and needn't reach their ends.
There are 2 independent parts, one for each index of `groups`. The reference program is written for one: setup_inputs(seed, part) draws one part's arguments, and reference() takes and returns one part's arrays. A program takes and returns all parts, laid end to end along the dimension named above; an argument that names none is the same for every part. Nothing has to cross between parts.
Inputs may be any that keep to these rules, and one draw needn't show every extreme that they name: The first 128 * cache_blocks[0] cached positions are valid.
All inputs are finite; a program needn't handle non-finite values.
Results may differ from the reference program's by a relative error of at most 0.019.
Values may be sent and summed in bfloat16 or wider, within the bound.
No kernel may reach another device: no remote copies, remote signals or barrier semaphores. Data moves between devices by JAX's collectives and lax.ppermute only.
A program may use at most 128 MiB of HBM per device.

```python
import jax
import jax.numpy as jnp
from jax import lax

D = 8192
HQ = 64
KVH = 8
DH = 128
FF = 14336
NEW = 128
BLOCK = 128
CACHE = 24576


def key_table(key):
    key_base = jax.random.truncated_normal(jax.random.fold_in(key, 11), -4.0, 4.0, (CACHE, KVH * DH), jnp.float32) * 1.7
    return key_base


def draw_cache_keys(key, part):
    key_base = key_table(key)
    return key_base.astype(jnp.bfloat16)


def draw_queries(key, part):
    query_key = jax.random.fold_in(key, 13)
    drawn = jax.random.truncated_normal(query_key, -4.0, 4.0, (NEW, HQ * DH), jnp.float32) * 1.7
    return drawn.astype(jnp.bfloat16)


def draw_residual(key, part):
    column = jnp.arange(D, dtype=jnp.float32) / D
    rough = jax.random.uniform(jax.random.fold_in(key, 21), (D,), jnp.float32, 0.7, 1.4)
    row_scale = 10.0 ** (0.5 * jax.random.uniform(jax.random.fold_in(key, 22), (NEW, 1), jnp.float32) - 0.25)
    noise = jax.random.truncated_normal(jax.random.fold_in(key, 23), -4.0, 4.0, (NEW, D), jnp.float32)
    column_scale = 10.0 ** (0.5 * column - 0.25)
    return (noise * column_scale * rough * row_scale).astype(jnp.bfloat16)


def steps_of(own_key, extent, shards, least, top_value):
    factor_of = 1.0
    for axis_at, shards_of in shards:
        draws = jax.random.uniform(jax.random.fold_in(jax.random.fold_in(own_key, 6), axis_at), (shards_of,), jnp.float32, least / len(shards), top_value / len(shards))
        factor_of = factor_of * jnp.repeat(jnp.exp(draws), extent[axis_at] // shards_of).reshape((-1,) + (1,) * (len(extent) - 1 - axis_at))
    return factor_of


def normal_values(own_key, shape, scale, bound, split=(), kind=jnp.bfloat16):
    result = scale * jax.random.normal(own_key, shape, jnp.float32)
    if split:
        result = result * steps_of(own_key, shape, split, -0.22, 0.18)
    return jnp.clip(result, -bound, bound).astype(kind)


def setup_inputs(seed: int = 0, part: int = 0) -> dict:
    keys = jax.random.split(jax.random.key(seed), 12)
    own_keys = jax.random.split(jax.random.fold_in(keys[11], part), 12)
    return {
        "queries": draw_queries(jax.random.fold_in(jax.random.fold_in(keys[11], part), 71), part),
        "cache_keys": draw_cache_keys(jax.random.fold_in(jax.random.fold_in(keys[11], part), 71), part),
        "cache_values": normal_values(own_keys[2], (CACHE, KVH * DH), 1.0, 6.0, ((0, 8), (1, 2))),
        "new_keys": normal_values(own_keys[3], (NEW, KVH * DH), 2.5, 10.0, ((0, 4), (1, 2))),
        "new_values": normal_values(own_keys[4], (NEW, KVH * DH), 1.0, 6.0, ((0, 4), (1, 2))),
        "cache_blocks": jax.random.randint(own_keys[5], (1,), CACHE // (4 * BLOCK), CACHE // BLOCK + 1).astype(jnp.int32),
        "residual": draw_residual(jax.random.fold_in(jax.random.fold_in(keys[11], part), 71), part),
        "norm_gain": jnp.clip(1.0 + 0.18 * jax.random.normal(keys[7], (D,), jnp.float32), 0.1, 1.9),
        "out_weight": normal_values(keys[8], (HQ * DH, D), (HQ * DH) ** -0.5, 0.0625, ((0, 2), (1, 8))),
        "gate_up": normal_values(keys[9], (D, 2, FF), D ** -0.5, 0.0625, ((0, 8), (2, 2))),
        "down_weight": normal_values(keys[10], (FF, D), FF ** -0.5, 0.046875, ((0, 2), (1, 8))),
    }


NEG = -1e+30

def reference(queries, cache_keys, cache_values, new_keys, new_values, cache_blocks, residual, norm_gain, out_weight, gate_up, down_weight):
    group_size = HQ // KVH
    valid_length = cache_blocks[0] * BLOCK
    cache_mask = jnp.arange(CACHE, dtype=jnp.int32) < valid_length
    token_index = jnp.arange(NEW, dtype=jnp.int32)
    self_mask = token_index[None, :] <= token_index[:, None]
    full_mask = jnp.concatenate([jnp.broadcast_to(cache_mask[None, :], (NEW, CACHE)), self_mask], axis=1)

    def one_head(head):
        column = (head // group_size * DH).astype(jnp.int32)
        query_cols = lax.dynamic_slice_in_dim(queries, (head * DH).astype(jnp.int32), DH, 1)
        key_rows = jnp.concatenate([lax.dynamic_slice_in_dim(cache_keys, column, DH, 1), lax.dynamic_slice_in_dim(new_keys, column, DH, 1)], axis=0)
        value_rows = jnp.concatenate([lax.dynamic_slice_in_dim(cache_values, column, DH, 1), lax.dynamic_slice_in_dim(new_values, column, DH, 1)], axis=0)
        scores = jnp.dot(query_cols, key_rows.T, preferred_element_type=jnp.float32) * DH ** (-0.5)
        scores = jnp.where(full_mask, scores, NEG)
        peak_score = lax.optimization_barrier(jnp.max(scores, axis=1, keepdims=True))
        weights = jnp.where(full_mask, jnp.exp(scores - peak_score), 0.0)
        weight_sum = lax.optimization_barrier(jnp.sum(weights, axis=1, keepdims=True))
        summed = jnp.dot(weights.astype(jnp.bfloat16), value_rows, preferred_element_type=jnp.float32)
        return (summed / weight_sum).astype(jnp.bfloat16)
    heads = lax.map(one_head, jnp.arange(HQ, dtype=jnp.int32))
    attention = jnp.transpose(heads, (1, 0, 2)).reshape(NEW, HQ * DH)
    projected = jnp.dot(attention, out_weight, preferred_element_type=jnp.float32)
    hidden_state = (residual.astype(jnp.float32) + projected).astype(jnp.bfloat16)
    values32 = hidden_state.astype(jnp.float32)
    mean_square = lax.optimization_barrier(jnp.mean(values32 * values32, axis=1, keepdims=True))
    normed = (values32 * lax.rsqrt(mean_square + 1e-05) * norm_gain).astype(jnp.bfloat16)
    both = jnp.dot(normed, gate_up.reshape(D, 2 * FF), preferred_element_type=jnp.float32)
    activated = (jax.nn.silu(both[:, :FF]) * both[:, FF:]).astype(jnp.bfloat16)
    down = jnp.dot(activated, down_weight, preferred_element_type=jnp.float32)
    return (values32 + down).astype(jnp.bfloat16)
```

```python
import functools

import jax
import jax.numpy as jnp
from jax import lax
from jax.experimental import pallas as pl
from jax.experimental.pallas import tpu as pltpu
from jax.sharding import PartitionSpec as P

D = 8192
HQ = 64
KVH = 8
DH = 128
BLOCK = 128


NEG = -1e30
EPSILON = 1e-05
CHUNK = 512
STREAMS = 2
TILE = 896


def shifted(value, axis, by):
    devices = lax.axis_size(axis)
    return lax.ppermute(value, axis, [(i, (i + by) % devices) for i in range(devices)])


def merged_2(value, axis, combine):
    everything = jax.tree.map(
        lambda part, kind: lax.all_gather(part.astype(kind), axis),
        value,
        jax.tree.map(lambda a: jnp.bfloat16 if a.dtype == jnp.float32 else a.dtype, value),
    )

    def take(k):
        return jax.tree.map(lambda part, own: part[k].astype(own.dtype), everything, value)

    return lax.fori_loop(
        1, lax.axis_size(axis), lambda k, so_far: combine(so_far, take(k)), take(0)
    )


def attend(query_block, key_block, value_block, allowed):
    row_count, local_groups, group_size, head_width = query_block.shape
    key_count = key_block.shape[0]
    keyed = key_block.reshape(key_count, local_groups, head_width)
    valued = value_block.reshape(key_count, local_groups, head_width)
    scores = jnp.einsum(
        "rkgd,nkd->rkgn", query_block, keyed, preferred_element_type=jnp.float32
    ) * head_width ** (-0.5)
    usable = allowed[:, None, None, :]
    scores = jnp.where(usable, scores, NEG)
    peak_score = jnp.max(scores, axis=3)
    weights = jnp.where(usable, jnp.exp(scores - peak_score[..., None]), 0.0)
    weight_sum = jnp.sum(weights, axis=3)
    summed = jnp.einsum(
        "rkgn,nkd->rkgd", weights.astype(jnp.bfloat16), valued, preferred_element_type=jnp.float32
    )
    return (summed, peak_score, weight_sum)


def combine(earlier_part, later_part):
    earlier_sum, earlier_peak, earlier_total = earlier_part
    later_sum, later_peak, later_total = later_part
    new_peak = jnp.maximum(earlier_peak, later_peak)
    earlier_scale = jnp.exp(earlier_peak - new_peak)
    later_scale = jnp.exp(later_peak - new_peak)
    return (
        earlier_sum * earlier_scale[..., None] + later_sum * later_scale[..., None],
        new_peak,
        earlier_total * earlier_scale + later_total * later_scale,
    )


def normalize(hidden_state, norm_gain):
    values32 = hidden_state.astype(jnp.float32)
    squares = lax.psum(jnp.sum(values32 * values32, axis=1), ("ctx", "khalf"))
    factor = lax.rsqrt(squares / D + EPSILON)
    return (values32 * factor[:, None] * norm_gain).astype(jnp.bfloat16)


def on_device_any(
    queries,
    cache_keys,
    cache_values,
    new_keys,
    new_values,
    cache_blocks,
    residual,
    norm_gain,
    out_weight,
    gate_up,
    down_weight,
):
    query_rows = queries.shape[0]
    group_size = HQ // KVH
    local_groups = cache_keys.shape[1] // DH
    local_queries = queries.reshape(query_rows, local_groups, group_size, DH)
    cache_length = cache_keys.shape[0]
    shard_index = lax.axis_index("ctx") * lax.axis_size("khalf") + lax.axis_index("khalf")
    positions = shard_index * cache_length + jnp.arange(cache_length, dtype=jnp.int32)
    cache_allowed = (positions < cache_blocks[0] * BLOCK)[None, :]
    query_start = lax.axis_index("ctx") * query_rows
    query_positions = query_start + jnp.arange(query_rows, dtype=jnp.int32)
    empty = (
        jnp.zeros((query_rows, local_groups, group_size, DH), jnp.float32),
        jnp.full((query_rows, local_groups, group_size), NEG, jnp.float32),
        jnp.zeros((query_rows, local_groups, group_size), jnp.float32),
    )

    def cycle_step(step_index, state_carry):
        visiting, partial_state = state_carry
        fresh = attend(visiting, cache_keys, cache_values, cache_allowed)
        partial_state = combine(partial_state, fresh)
        visiting = shifted(visiting, "ctx", 1)
        partial_state = (
            shifted(partial_state[0].astype(jnp.bfloat16), "ctx", 1).astype(jnp.float32),
            shifted(partial_state[1].astype(jnp.bfloat16), "ctx", 1).astype(jnp.float32),
            shifted(partial_state[2].astype(jnp.bfloat16), "ctx", 1).astype(jnp.float32),
        )
        return (visiting, partial_state)

    returned, cache_part = lax.fori_loop(
        0, lax.axis_size("ctx"), cycle_step, (local_queries, empty)
    )
    merged = merged_2(cache_part, "khalf", combine)
    piece_keys = lax.all_gather(new_keys, "ctx", axis=0, tiled=True)
    piece_values = lax.all_gather(new_values, "ctx", axis=0, tiled=True)
    key_positions = jnp.arange(piece_keys.shape[0], dtype=jnp.int32)
    allowed = key_positions[None, :] <= query_positions[:, None]
    own_part = combine(empty, attend(local_queries, piece_keys, piece_values, allowed))
    joined = combine(merged, own_part)
    attention = (
        (joined[0] / joined[2][..., None])
        .astype(jnp.bfloat16)
        .reshape(query_rows, local_groups * group_size * DH)
    )
    partial_rows = jnp.dot(
        lax.all_gather(attention, "ctx", axis=0, tiled=True),
        out_weight,
        preferred_element_type=jnp.float32,
    )
    projected = lax.psum(partial_rows.astype(jnp.bfloat16), "kv").astype(jnp.float32)
    hidden_state = (residual.astype(jnp.float32) + projected).astype(jnp.bfloat16)
    normed = normalize(hidden_state, norm_gain)
    own_rows = hidden_state.shape[0] // lax.axis_size("kv")
    kept = lax.dynamic_slice_in_dim(hidden_state, lax.axis_index("kv") * own_rows, own_rows, 0)
    local_width = gate_up.shape[0]
    local_hidden = gate_up.shape[2]
    merged_weight = gate_up.reshape(local_width, 2 * local_hidden)
    both = lax.psum_scatter(
        jnp.dot(normed, merged_weight, preferred_element_type=jnp.float32).astype(jnp.bfloat16),
        ("ctx", "khalf"),
        scatter_dimension=0,
        tiled=True,
    ).astype(jnp.float32)
    activated = (jax.nn.silu(both[:, :local_hidden]) * both[:, local_hidden:]).astype(jnp.bfloat16)
    partial_out = jnp.dot(
        lax.all_gather(activated, ("ctx", "khalf"), axis=0, tiled=True),
        down_weight,
        preferred_element_type=jnp.float32,
    )
    down = lax.psum_scatter(
        partial_out.astype(jnp.bfloat16), "kv", scatter_dimension=0, tiled=True
    ).astype(jnp.float32)
    return (kept.astype(jnp.float32) + down).astype(jnp.bfloat16)


LOG2E = 1.4426950408889634
PIECES = 3
STAT_ROWS = 16


def rotation(value, axis, by):
    devices = lax.axis_size(axis)
    return lax.ppermute(value, axis, [(i, (i + by) % devices) for i in range(devices)])


def exchanged(value, axis, bit):
    devices = lax.axis_size(axis)
    return lax.ppermute(value, axis, [(i, i ^ bit) for i in range(devices)])


def identity_mask(size):
    rows = lax.broadcasted_iota(jnp.int32, (size, size), 0)
    columns = lax.broadcasted_iota(jnp.int32, (size, size), 1)
    return rows == columns


def column_to_row(column, eye):
    return jnp.sum(jnp.where(eye, jnp.broadcast_to(column, eye.shape), 0.0), axis=0, keepdims=True)


def row_to_column(row, eye):
    return jnp.sum(jnp.where(eye, jnp.broadcast_to(row, eye.shape), 0.0), axis=1, keepdims=True)


def store_payload(ref, outs, lse_rows):
    count = len(outs)
    for at, block in enumerate(outs):
        ref[at * 128 : (at + 1) * 128, :] = block.astype(jnp.bfloat16)
    stats = jnp.concatenate(lse_rows, axis=0)
    high = stats.astype(jnp.bfloat16)
    rest = stats - high.astype(jnp.float32)
    middle = rest.astype(jnp.bfloat16)
    low = (rest - middle.astype(jnp.float32)).astype(jnp.bfloat16)
    pieces = [p.astype(jnp.float32) for p in (high, middle, low)]
    pad = jnp.zeros((STAT_ROWS - PIECES * count, 128), jnp.float32)
    ref[count * 128 : count * 128 + STAT_ROWS, :] = jnp.concatenate(pieces + [pad], axis=0).astype(
        jnp.bfloat16
    )


def attention_kernel(
    scal_ref,
    q_mine_ref,
    q_other_ref,
    k_hbm,
    v_hbm,
    nk_ref,
    nv_ref,
    keep_ref,
    send_ref,
    k_buf,
    v_buf,
    q_buf,
    s_buf,
    max_buf,
    sum_buf,
    acc_buf,
    k_sem,
    v_sem,
    *,
    chunk,
    group_size,
):
    core = scal_ref[0]
    valid = scal_ref[1]
    new_offset = scal_ref[2]
    rows_in = q_mine_ref.shape[0]
    pair = q_mine_ref.shape[1] // (group_size * DH)
    rows = rows_in * group_size
    factor = DH ** (-0.5) * LOG2E
    whole_chunks = valid // chunk
    some_left = valid - whole_chunks * chunk
    chunks = whole_chunks + jnp.where(some_left > 0, 1, 0)

    def key_copy(c):
        at = pl.multiple_of(c * chunk, chunk)
        return pltpu.make_async_copy(
            k_hbm.at[pl.ds(at, chunk), :], k_buf.at[pl.ds(at, chunk), :], k_sem.at[c]
        )

    def value_copy(c):
        at = pl.multiple_of(c * chunk, chunk)
        return pltpu.make_async_copy(
            v_hbm.at[pl.ds(at, chunk), :], v_buf.at[pl.ds(at, chunk), :], v_sem.at[c]
        )

    def start_keys(c, carry):
        key_copy(c).start()
        return carry

    def start_values(c, carry):
        value_copy(c).start()
        return carry

    lax.fori_loop(0, chunks, start_keys, 0)
    lax.fori_loop(0, chunks, start_values, 0)

    def column_of(j):
        owner = core if j < pair else 1 - core
        return pl.multiple_of((owner * pair + j % pair) * DH, DH)

    new_masks = (
        lax.broadcasted_iota(jnp.int32, (rows, nk_ref.shape[0]), 1)
        <= lax.broadcasted_iota(jnp.int32, (rows, nk_ref.shape[0]), 0) % rows_in + new_offset
    )
    new_scores = []
    for j in range(2 * pair):
        ref = q_mine_ref if j < pair else q_other_ref
        base = (j % pair) * group_size * DH
        q_buf[j] = jnp.concatenate(
            [ref[:, base + h * DH : base + (h + 1) * DH] for h in range(group_size)], axis=0
        )
        fresh = lax.dot_general(
            q_buf[j],
            nk_ref[:, pl.ds(column_of(j), DH)],
            (((1,), (1,)), ((), ())),
            preferred_element_type=jnp.float32,
        )
        new_scores.append(jnp.where(new_masks, fresh, NEG))
    max_buf[...] = jnp.full(max_buf.shape, NEG, jnp.float32)
    sum_buf[...] = jnp.zeros(sum_buf.shape, jnp.float32)
    acc_buf[...] = jnp.zeros(acc_buf.shape, jnp.float32)

    def scores_of(c, masked):
        key_copy(c).wait()
        at = pl.multiple_of(c * chunk, chunk)
        for j in range(2 * pair):
            scores = lax.dot_general(
                q_buf[j],
                k_buf[pl.ds(at, chunk), pl.ds(column_of(j), DH)],
                (((1,), (1,)), ((), ())),
                preferred_element_type=jnp.float32,
            )
            if masked:
                places = lax.broadcasted_iota(jnp.int32, scores.shape, 1)
                scores = jnp.where(places < some_left, scores, NEG)
            s_buf[j, :, pl.ds(at, chunk)] = scores
            top = max_buf[j]
            for part in range(chunk // 128):
                top = jnp.maximum(top, scores[:, part * 128 : (part + 1) * 128])
            max_buf[j] = top

    def whole_step(c, carry):
        scores_of(c, False)
        return carry

    lax.fori_loop(0, whole_chunks, whole_step, 0)

    @pl.when(some_left > 0)
    def _():
        scores_of(whole_chunks, True)

    peaks = []
    for j in range(2 * pair):
        peak = jnp.max(max_buf[j], axis=1, keepdims=True)
        peak = jnp.maximum(peak, jnp.max(new_scores[j], axis=1, keepdims=True))
        peaks.append(peak * factor)

    def weights_step(c, carry):
        value_copy(c).wait()
        at = pl.multiple_of(c * chunk, chunk)
        for j in range(2 * pair):
            weights = jnp.exp2(s_buf[j, :, pl.ds(at, chunk)] * factor - peaks[j])
            total = sum_buf[j]
            for part in range(chunk // 128):
                total = total + weights[:, part * 128 : (part + 1) * 128]
            sum_buf[j] = total
            acc_buf[j] += jnp.dot(
                weights.astype(jnp.bfloat16),
                v_buf[pl.ds(at, chunk), pl.ds(column_of(j), DH)],
                preferred_element_type=jnp.float32,
            )
        return carry

    lax.fori_loop(0, chunks, weights_step, 0)
    eye = identity_mask(128)
    for ref, first in ((keep_ref, 0), (send_ref, pair)):
        outs = []
        lse_rows = []
        for j in range(first, first + pair):
            weights = jnp.where(
                new_masks, jnp.exp2(new_scores[j] * factor - peaks[j]), 0.0
            )
            total = jnp.sum(sum_buf[j], axis=1, keepdims=True) + jnp.sum(
                weights, axis=1, keepdims=True
            )
            summed = acc_buf[j] + jnp.dot(
                weights.astype(jnp.bfloat16),
                nv_ref[:, pl.ds(column_of(j), DH)],
                preferred_element_type=jnp.float32,
            )
            filled = total > 0.0
            safe = jnp.where(filled, total, 1.0)
            lse = jnp.where(filled, peaks[j] + jnp.log(safe) * LOG2E, NEG)
            result = summed / safe
            for part in range(rows // 128):
                span = slice(part * 128, (part + 1) * 128)
                outs.append(result[span])
                lse_rows.append(column_to_row(lse[span], eye))
        store_payload(ref, outs, lse_rows)


def merge_kernel(*refs, final, rows_in):
    parts, out_ref = refs[:-1], refs[-1]
    blocks = (parts[0].shape[0] - STAT_ROWS) // 128
    eye = identity_mask(128)
    lses = []
    for ref in parts:
        stats = ref[blocks * 128 : blocks * 128 + STAT_ROWS, :].astype(jnp.float32)
        lse = stats[0:blocks]
        for piece in range(1, PIECES):
            lse = lse + stats[piece * blocks : (piece + 1) * blocks]
        lses.append(lse)
    peak = lses[0]
    for lse in lses[1:]:
        peak = jnp.maximum(peak, lse)
    shares = [jnp.exp2(lse - peak) for lse in lses]
    total = shares[0]
    for share in shares[1:]:
        total = total + share
    outs = []
    for at in range(blocks):
        mixed = None
        for ref, share in zip(parts, shares):
            scale = row_to_column((share / total)[at : at + 1], eye)
            term = ref[at * 128 : (at + 1) * 128, :].astype(jnp.float32) * scale
            mixed = term if mixed is None else mixed + term
        outs.append(mixed)
    if not final:
        merged = peak + jnp.log(total) * LOG2E
        store_payload(out_ref, outs, [merged[at : at + 1] for at in range(blocks)])
        return
    heads_in = 128 // rows_in
    for at in range(blocks):
        for h in range(heads_in):
            head = at * heads_in + h
            out_ref[:, head * DH : (head + 1) * DH] = outs[at][
                h * rows_in : (h + 1) * rows_in
            ].astype(jnp.bfloat16)


def projection_kernel(scal_ref, *refs, devices):
    mine, other = refs[:devices], refs[devices : 2 * devices]
    weight_ref, out_ref, left_buf = refs[2 * devices :]
    core = scal_ref[0]
    rows, half = mine[0].shape

    @pl.when(pl.program_id(0) == 0)
    def _():
        for s in range(devices):
            at = pl.multiple_of(scal_ref[1 + s] * rows, rows)
            left_buf[pl.ds(at, rows), pl.ds(pl.multiple_of(core * half, half), half)] = mine[s][...]
            left_buf[pl.ds(at, rows), pl.ds(pl.multiple_of((1 - core) * half, half), half)] = other[
                s
            ][...]

    out_ref[...] = jnp.dot(
        left_buf[...], weight_ref[...], preferred_element_type=jnp.float32
    ).astype(jnp.bfloat16)


def prepare_kernel(scal_ref, residual_ref, own_ref, other_ref, gain_ref, hidden_ref, left_ref, squares_ref):
    core = scal_ref[0]
    rows, width = residual_ref.shape
    half = rows // 2
    values = (
        residual_ref[...].astype(jnp.float32)
        + own_ref[...].astype(jnp.float32)
        + other_ref[...].astype(jnp.float32)
    )
    hidden = values.astype(jnp.bfloat16)
    hidden_ref[...] = hidden
    values = hidden.astype(jnp.float32)
    squares = jnp.sum(values * values, axis=1, keepdims=True)
    squares_ref[...] = jnp.broadcast_to(column_to_row(squares, identity_mask(rows)), squares_ref.shape)
    gained = (values * gain_ref[...]).astype(jnp.bfloat16)
    low, high = gained[:half], gained[half:]
    keep = jnp.where(core == 0, low, high)
    send = jnp.where(core == 0, high, low)
    places = lax.broadcasted_iota(jnp.int32, (128, 256), 0) * 2
    spots = lax.broadcasted_iota(jnp.int32, (128, 256), 1)
    spread = [jnp.where(spots == places + s, 1.0, 0.0).astype(jnp.bfloat16) for s in (0, 1)]
    for k in range(width // 128):
        for at, source in ((0, keep), (2, send)):
            for s in (0, 1):
                left_ref[(at + s) * half : (at + s + 1) * half, k * 256 : (k + 1) * 256] = jnp.dot(
                    source[:, k * 128 : (k + 1) * 128], spread[s], preferred_element_type=jnp.float32
                ).astype(jnp.bfloat16)


def gate_up_kernel(left_ref, weight_ref, keep_ref, send_ref):
    rows = keep_ref.shape[0]
    depth, two, width = weight_ref.shape
    merged_weight = weight_ref.reshape(depth * two, width)[...]
    both = jnp.dot(left_ref[...], merged_weight, preferred_element_type=jnp.float32)
    keep_ref[...] = both[:rows].astype(jnp.bfloat16)
    send_ref[...] = both[rows:].astype(jnp.bfloat16)


def activation_kernel(scal_ref, own_ref, other_ref, squares_ref, out_ref):
    core = scal_ref[0]
    half = out_ref.shape[0]
    total = 2 * half
    both = own_ref[...].astype(jnp.float32) + other_ref[...].astype(jnp.float32)
    factor = lax.rsqrt(squares_ref[0:1, :] / D + EPSILON)
    column = row_to_column(factor, identity_mask(total))
    column = jnp.where(core == 0, column[:half], column[half:])
    gate = both[:half] * column
    up = both[half:] * column
    out_ref[...] = (gate / (1.0 + jnp.exp(-gate)) * up).astype(jnp.bfloat16)


def down_kernel(scal_ref, *refs, pieces):
    mine, other = refs[:pieces], refs[pieces : 2 * pieces]
    weight_ref, keep_ref, send_ref, acc_buf = refs[2 * pieces :]
    core = scal_ref[0]
    side = scal_ref[1]
    half = mine[0].shape[0]
    step = pl.program_id(0)

    @pl.when(step == 0)
    def _():
        acc_buf[...] = jnp.zeros(acc_buf.shape, jnp.float32)

    for s in range(pieces):

        @pl.when(step == s)
        def _(s=s):
            first = mine[s][...]
            second = other[s][...]
            left = jnp.concatenate(
                [jnp.where(core == 0, first, second), jnp.where(core == 0, second, first)], axis=0
            )
            acc_buf[...] += jnp.dot(left, weight_ref[...], preferred_element_type=jnp.float32)

    @pl.when(step == pieces - 1)
    def _():
        keep_ref[...] = acc_buf[pl.ds(pl.multiple_of(side * half, half), half), :]
        send_ref[...] = acc_buf[pl.ds(pl.multiple_of((1 - side) * half, half), half), :].astype(
            jnp.bfloat16
        )


def vmem():
    return pl.BlockSpec(memory_space=pltpu.VMEM)


def smem():
    return pl.BlockSpec(memory_space=pltpu.SMEM)


def cost(flops, size):
    return pl.CostEstimate(flops=int(flops), bytes_accessed=int(size), transcendentals=0)


def attend_visiting(scal, q_mine, q_other, cache_keys, cache_values, new_keys, new_values, group_size):
    length, width = cache_keys.shape
    rows_in = q_mine.shape[0]
    groups = width // DH
    rows = rows_in * group_size
    chunk = CHUNK
    payload = jax.ShapeDtypeStruct((groups // 2 * rows + STAT_ROWS, DH), jnp.bfloat16)
    return pl.pallas_call(
        functools.partial(attention_kernel, chunk=chunk, group_size=group_size),
        out_shape=(payload, payload),
        in_specs=[
            smem(),
            vmem(),
            vmem(),
            pl.BlockSpec(memory_space=pl.ANY),
            pl.BlockSpec(memory_space=pl.ANY),
            vmem(),
            vmem(),
        ],
        out_specs=(vmem(), vmem()),
        scratch_shapes=[
            pltpu.VMEM((length, width), jnp.bfloat16),
            pltpu.VMEM((length, width), jnp.bfloat16),
            pltpu.VMEM((groups, rows, DH), jnp.bfloat16),
            pltpu.VMEM((groups, rows, length), jnp.float32),
            pltpu.VMEM((groups, rows, 128), jnp.float32),
            pltpu.VMEM((groups, rows, 128), jnp.float32),
            pltpu.VMEM((groups, rows, DH), jnp.float32),
            pltpu.SemaphoreType.DMA((length // chunk,)),
            pltpu.SemaphoreType.DMA((length // chunk,)),
        ],
        compiler_params=pltpu.CompilerParams(vmem_limit_bytes=40 * 2**20),
        cost_estimate=cost(4 * groups * rows * length * DH, 4 * length * width),
        name="attend",
    )(scal, q_mine, q_other, cache_keys, cache_values, new_keys, new_values)


def merged(parts, final, rows_in):
    blocks = (parts[0].shape[0] - STAT_ROWS) // 128
    if final:
        shape = (rows_in, blocks * 128 // rows_in * DH)
    else:
        shape = parts[0].shape
    return pl.pallas_call(
        functools.partial(merge_kernel, final=final, rows_in=rows_in),
        out_shape=jax.ShapeDtypeStruct(shape, jnp.bfloat16),
        in_specs=[vmem()] * len(parts),
        out_specs=vmem(),
        cost_estimate=cost(blocks * 128 * 128 * 8 * len(parts), parts[0].size * 2 * len(parts)),
        name="merge",
    )(*parts)


def project(scal, mine, other, weight):
    devices = len(mine)
    rows = mine[0].shape[0] * devices
    depth, width = weight.shape
    tile = 256
    return pl.pallas_call(
        functools.partial(projection_kernel, devices=devices),
        grid=(width // tile,),
        out_shape=jax.ShapeDtypeStruct((rows, width), jnp.bfloat16),
        in_specs=[smem()]
        + [pl.BlockSpec(a.shape, lambda i: (0, 0)) for a in (*mine, *other)]
        + [pl.BlockSpec((depth, tile), lambda i: (0, i))],
        out_specs=pl.BlockSpec((rows, tile), lambda i: (0, i)),
        scratch_shapes=[pltpu.VMEM((rows, depth), jnp.bfloat16)],
        cost_estimate=cost(2 * rows * depth * width, 2 * depth * width),
        name="project",
    )(scal, *mine, *other, weight)


def prepare(scal, residual, own, other, gain):
    rows, width = residual.shape
    return pl.pallas_call(
        prepare_kernel,
        out_shape=(
            jax.ShapeDtypeStruct((rows, width), jnp.bfloat16),
            jax.ShapeDtypeStruct((2 * rows, 2 * width), jnp.bfloat16),
            jax.ShapeDtypeStruct((8, rows), jnp.float32),
        ),
        in_specs=[smem()] + [vmem()] * 4,
        out_specs=(vmem(),) * 3,
        cost_estimate=cost(rows * width * 1024, rows * width * 8),
        name="prepare",
    )(scal, residual, own, other, gain.reshape(1, width))


def gate_up_part(left, weight, start, count, tile):
    rows2, depth2 = left.shape
    depth = depth2 // 2
    rows = rows2 // 2
    first = start // tile
    out = jax.ShapeDtypeStruct((rows, count), jnp.bfloat16)
    return pl.pallas_call(
        gate_up_kernel,
        grid=(count // tile,),
        out_shape=(out, out),
        in_specs=[
            pl.BlockSpec((rows2, depth2), lambda i: (0, 0)),
            pl.BlockSpec((depth, 2, tile), lambda i: (0, 0, first + i)),
        ],
        out_specs=(
            pl.BlockSpec((rows, tile), lambda i: (0, i)),
            pl.BlockSpec((rows, tile), lambda i: (0, i)),
        ),
        cost_estimate=cost(2 * rows2 * depth2 * count, 4 * depth * count),
        name="gate_up",
    )(left, weight)


def activate(scal, own, other, squares):
    rows, width = own.shape
    return pl.pallas_call(
        activation_kernel,
        out_shape=jax.ShapeDtypeStruct((rows // 2, width), jnp.bfloat16),
        in_specs=[smem()] + [vmem()] * 3,
        out_specs=vmem(),
        cost_estimate=cost(rows * width * 16, rows * width * 5),
        name="activate",
    )(scal, own, other, squares)


def down_project(scal, mine, other, weight):
    pieces = len(mine)
    half, tile = mine[0].shape
    width = weight.shape[1]
    return pl.pallas_call(
        functools.partial(down_kernel, pieces=pieces),
        grid_spec=pltpu.PrefetchScalarGridSpec(
            num_scalar_prefetch=1,
            grid=(pieces,),
            in_specs=[pl.BlockSpec((half, tile), lambda i, s: (0, 0)) for _ in range(2 * pieces)]
            + [pl.BlockSpec((tile, width), lambda i, s: (s[2 + i], 0))],
            out_specs=(
                pl.BlockSpec((half, width), lambda i, s: (0, 0)),
                pl.BlockSpec((half, width), lambda i, s: (0, 0)),
            ),
            scratch_shapes=[pltpu.VMEM((2 * half, width), jnp.float32)],
        ),
        out_shape=(
            jax.ShapeDtypeStruct((half, width), jnp.float32),
            jax.ShapeDtypeStruct((half, width), jnp.bfloat16),
        ),
        cost_estimate=cost(4 * half * tile * pieces * width, 2 * pieces * tile * width),
        name="down",
    )(scal, *mine, *other, weight)


def half_of(value, which, axis=1):
    size = value.shape[axis] // 2
    return lax.dynamic_slice_in_dim(value, which * size, size, axis)


def added(a, b):
    return (a.astype(jnp.float32) + b.astype(jnp.float32)).astype(jnp.bfloat16)


def on_device_line(
    queries,
    cache_keys,
    cache_values,
    new_keys,
    new_values,
    cache_blocks,
    residual,
    norm_gain,
    out_weight,
    gate_up,
    down_weight,
):
    devices = lax.axis_size("ctx")
    place = lax.axis_index("ctx")
    core = lax.axis_index("khalf")
    side = lax.axis_index("kv")
    group_size = HQ // KVH
    rows_in = queries.shape[0]
    length = cache_keys.shape[0]
    shard = place * 2 + core
    valid = jnp.clip(cache_blocks[0] * BLOCK - shard * length, 0, length).astype(jnp.int32)
    q_mine = half_of(queries, core)
    q_other = half_of(queries, 1 - core)

    def visit(block, mine, other):
        offset = jnp.where(core == 0, (block - place) * rows_in, -(2**24))
        scal = jnp.stack([core, valid, offset]).astype(jnp.int32)
        keep, send = attend_visiting(
            scal, mine, other, cache_keys, cache_values, new_keys, new_values, group_size
        )
        return merged([keep, exchanged(send, "khalf", 1)], False, rows_in)

    visiting = [rotation(q_mine, "ctx", s) for s in range(1, devices)]
    parts = [visit(place, q_mine, q_other)]
    for s in range(1, devices):
        mine = visiting[s - 1]
        part = visit((place - s) % devices, mine, exchanged(mine, "khalf", 1))
        parts.append(rotation(part, "ctx", -s))
    attention = merged(parts, True, rows_in)
    mine = [attention] + [rotation(attention, "ctx", s) for s in range(1, devices)]
    other = [exchanged(a, "khalf", 1) for a in mine]
    sources = [(place - s) % devices for s in range(devices)]
    partial = project(jnp.stack([core, *sources]).astype(jnp.int32), mine, other, out_weight)
    core_scal = jnp.stack([core, side]).astype(jnp.int32)
    hidden, left, squares = prepare(
        core_scal, residual, partial, exchanged(partial, "kv", 1), norm_gain
    )
    squares = squares + exchanged(squares, "khalf", 1)
    bits = [1 << b for b in range(devices.bit_length() - 1)]
    for bit in bits:
        squares = squares + exchanged(squares, "ctx", bit)
    hidden_width = gate_up.shape[2]
    span = hidden_width // STREAMS
    mine, other = [], []
    blocks = []
    for stream in range(STREAMS):
        keep, send = gate_up_part(left, gate_up, stream * span, span, TILE)
        come = exchanged(send, "khalf", 1)
        for bit in bits:
            upper = (place // bit) % 2
            away = added(half_of(keep, 1 - upper), half_of(come, 1 - upper))
            keep = added(half_of(keep, upper), half_of(come, upper))
            come = exchanged(away, "ctx", bit)
        activated = activate(core_scal, keep, come, squares)
        for s in range(devices):
            piece = activated if s == 0 else rotation(activated, "ctx", s)
            mine.append(piece)
            other.append(exchanged(piece, "khalf", 1))
            source = (place - s) % devices
            at = stream * devices
            for b, bit in enumerate(bits):
                at = at + (source // bit) % 2 * (devices >> (b + 1))
            blocks.append(at)
    down_scal = jnp.stack([core, side, *blocks]).astype(jnp.int32)
    keep, send = down_project(down_scal, mine, other, down_weight)
    come = exchanged(send, "kv", 1)
    kept = half_of(hidden, side, 0)
    return (kept.astype(jnp.float32) + keep + come.astype(jnp.float32)).astype(jnp.bfloat16)


def line_fits(mesh, keys_shape, hidden_width):
    sizes = dict(mesh.shape)
    ctx, kv, khalf = sizes["ctx"], sizes["kv"], sizes["khalf"]
    groups = keys_shape[1] // kv // DH
    length = keys_shape[0] // (sizes["groups"] * ctx * khalf)
    return (
        ctx & (ctx - 1) == 0
        and kv == 2
        and khalf == 2
        and groups % 2 == 0
        and length % CHUNK == 0
        and hidden_width // kv % (STREAMS * ctx * 128) == 0
        and hidden_width // kv // STREAMS % TILE == 0
    )


def solution(mesh):
    def on_device(*arguments):
        keys, gate_up = arguments[1], arguments[9]
        sizes = dict(mesh.shape)
        keys_shape = (
            keys.shape[0] * sizes["groups"] * sizes["ctx"] * sizes["khalf"],
            keys.shape[1] * sizes["kv"],
        )
        if line_fits(mesh, keys_shape, gate_up.shape[2] * sizes["kv"]):
            return on_device_line(*arguments)
        return on_device_any(*arguments)

    in_specs = (
        P(("groups", "ctx"), "kv"),
        P(("groups", "ctx", "khalf"), "kv"),
        P(("groups", "ctx", "khalf"), "kv"),
        P(("groups", "ctx"), "kv"),
        P(("groups", "ctx"), "kv"),
        P("groups"),
        P("groups", ("ctx", "khalf")),
        P(("ctx", "khalf")),
        P("kv", ("ctx", "khalf")),
        P(("ctx", "khalf"), None, "kv"),
        P("kv", ("ctx", "khalf")),
    )
    out_specs = P(("groups", "kv"), ("ctx", "khalf"))
    return jax.shard_map(
        on_device, mesh=mesh, in_specs=in_specs, out_specs=out_specs, check_vma=False
    )
```

```python
import functools

import jax
import jax.numpy as jnp
from jax import lax
from jax.experimental import pallas as pl
from jax.experimental.pallas import tpu as pltpu
from jax.sharding import PartitionSpec as P


D = 8192
HQ = 64
KVH = 8
DH = 128
BLOCK = 128


NEG = -1e30
EPSILON = 1e-05
STREAMS = (4, 3)
SLABS = 2


def shifted(value, axis, by):
    devices = lax.axis_size(axis)
    return lax.ppermute(value, axis, [(i, (i + by) % devices) for i in range(devices)])


def merged_2(value, axis, combine):
    everything = jax.tree.map(
        lambda part, kind: lax.all_gather(part.astype(kind), axis),
        value,
        jax.tree.map(lambda a: jnp.bfloat16 if a.dtype == jnp.float32 else a.dtype, value),
    )

    def take(k):
        return jax.tree.map(lambda part, own: part[k].astype(own.dtype), everything, value)

    return lax.fori_loop(
        1, lax.axis_size(axis), lambda k, so_far: combine(so_far, take(k)), take(0)
    )


def attend(query_block, key_block, value_block, allowed):
    _, local_groups, _, head_width = query_block.shape
    key_count = key_block.shape[0]
    keyed = key_block.reshape(key_count, local_groups, head_width)
    valued = value_block.reshape(key_count, local_groups, head_width)
    scores = jnp.einsum(
        "rkgd,nkd->rkgn", query_block, keyed, preferred_element_type=jnp.float32
    ) * head_width ** (-0.5)
    usable = allowed[:, None, None, :]
    scores = jnp.where(usable, scores, NEG)
    peak_score = jnp.max(scores, axis=3)
    weights = jnp.where(usable, jnp.exp(scores - peak_score[..., None]), 0.0)
    weight_sum = jnp.sum(weights, axis=3)
    summed = jnp.einsum(
        "rkgn,nkd->rkgd", weights.astype(jnp.bfloat16), valued, preferred_element_type=jnp.float32
    )
    return (summed, peak_score, weight_sum)


def combine(earlier_part, later_part):
    earlier_sum, earlier_peak, earlier_total = earlier_part
    later_sum, later_peak, later_total = later_part
    new_peak = jnp.maximum(earlier_peak, later_peak)
    earlier_scale = jnp.exp(earlier_peak - new_peak)
    later_scale = jnp.exp(later_peak - new_peak)
    return (
        earlier_sum * earlier_scale[..., None] + later_sum * later_scale[..., None],
        new_peak,
        earlier_total * earlier_scale + later_total * later_scale,
    )


def normalize(hidden_state, norm_gain):
    values32 = hidden_state.astype(jnp.float32)
    squares = lax.psum(jnp.sum(values32 * values32, axis=1), ("ctx", "khalf"))
    factor = lax.rsqrt(squares / D + EPSILON)
    return (values32 * factor[:, None] * norm_gain).astype(jnp.bfloat16)


def on_device_any(
    queries,
    cache_keys,
    cache_values,
    new_keys,
    new_values,
    cache_blocks,
    residual,
    norm_gain,
    out_weight,
    gate_up,
    down_weight,
):
    query_rows = queries.shape[0]
    group_size = HQ // KVH
    local_groups = cache_keys.shape[1] // DH
    local_queries = queries.reshape(query_rows, local_groups, group_size, DH)
    cache_length = cache_keys.shape[0]
    shard_index = lax.axis_index("ctx") * lax.axis_size("khalf") + lax.axis_index("khalf")
    positions = shard_index * cache_length + jnp.arange(cache_length, dtype=jnp.int32)
    cache_allowed = (positions < cache_blocks[0] * BLOCK)[None, :]
    query_start = lax.axis_index("ctx") * query_rows
    query_positions = query_start + jnp.arange(query_rows, dtype=jnp.int32)
    empty = (
        jnp.zeros((query_rows, local_groups, group_size, DH), jnp.float32),
        jnp.full((query_rows, local_groups, group_size), NEG, jnp.float32),
        jnp.zeros((query_rows, local_groups, group_size), jnp.float32),
    )

    def cycle_step(step_index, state_carry):
        visiting, partial_state = state_carry
        fresh = attend(visiting, cache_keys, cache_values, cache_allowed)
        partial_state = combine(partial_state, fresh)
        visiting = shifted(visiting, "ctx", 1)
        partial_state = (
            shifted(partial_state[0].astype(jnp.bfloat16), "ctx", 1).astype(jnp.float32),
            shifted(partial_state[1].astype(jnp.bfloat16), "ctx", 1).astype(jnp.float32),
            shifted(partial_state[2].astype(jnp.bfloat16), "ctx", 1).astype(jnp.float32),
        )
        return (visiting, partial_state)

    _, cache_part = lax.fori_loop(0, lax.axis_size("ctx"), cycle_step, (local_queries, empty))
    merged = merged_2(cache_part, "khalf", combine)
    piece_keys = lax.all_gather(new_keys, "ctx", axis=0, tiled=True)
    piece_values = lax.all_gather(new_values, "ctx", axis=0, tiled=True)
    key_positions = jnp.arange(piece_keys.shape[0], dtype=jnp.int32)
    allowed = key_positions[None, :] <= query_positions[:, None]
    own_part = combine(empty, attend(local_queries, piece_keys, piece_values, allowed))
    joined = combine(merged, own_part)
    attention = (
        (joined[0] / joined[2][..., None])
        .astype(jnp.bfloat16)
        .reshape(query_rows, local_groups * group_size * DH)
    )
    partial_rows = jnp.dot(
        lax.all_gather(attention, "ctx", axis=0, tiled=True),
        out_weight,
        preferred_element_type=jnp.float32,
    )
    projected = lax.psum(partial_rows.astype(jnp.bfloat16), "kv").astype(jnp.float32)
    hidden_state = (residual.astype(jnp.float32) + projected).astype(jnp.bfloat16)
    normed = normalize(hidden_state, norm_gain)
    own_rows = hidden_state.shape[0] // lax.axis_size("kv")
    kept = lax.dynamic_slice_in_dim(hidden_state, lax.axis_index("kv") * own_rows, own_rows, 0)
    local_width = gate_up.shape[0]
    local_hidden = gate_up.shape[2]
    merged_weight = gate_up.reshape(local_width, 2 * local_hidden)
    both = lax.psum_scatter(
        jnp.dot(normed, merged_weight, preferred_element_type=jnp.float32).astype(jnp.bfloat16),
        ("ctx", "khalf"),
        scatter_dimension=0,
        tiled=True,
    ).astype(jnp.float32)
    activated = (jax.nn.silu(both[:, :local_hidden]) * both[:, local_hidden:]).astype(jnp.bfloat16)
    partial_out = jnp.dot(
        lax.all_gather(activated, ("ctx", "khalf"), axis=0, tiled=True),
        down_weight,
        preferred_element_type=jnp.float32,
    )
    down = lax.psum_scatter(
        partial_out.astype(jnp.bfloat16), "kv", scatter_dimension=0, tiled=True
    ).astype(jnp.float32)
    return (kept.astype(jnp.float32) + down).astype(jnp.bfloat16)


LOG2E = 1.4426950408889634
PIECES = 3
STAT_ROWS = 16
SMALL = 8 * 2**20
MEDIUM = 16 * 2**20
LARGE = 28 * 2**20
ALONE = 61 * 2**20
LOADING = 12 * 2**20
LANES = 4


def rotation(value, axis, by):
    devices = lax.axis_size(axis)
    return lax.ppermute(value, axis, [(i, (i + by) % devices) for i in range(devices)])


def exchanged(value, axis, bit):
    devices = lax.axis_size(axis)
    return lax.ppermute(value, axis, [(i, i ^ bit) for i in range(devices)])


def identity_mask(size):
    rows = lax.broadcasted_iota(jnp.int32, (size, size), 0)
    columns = lax.broadcasted_iota(jnp.int32, (size, size), 1)
    return rows == columns


def column_to_row(column, eye):
    return jnp.sum(jnp.where(eye, jnp.broadcast_to(column, eye.shape), 0.0), axis=0, keepdims=True)


def row_to_column(row, eye):
    return jnp.sum(jnp.where(eye, jnp.broadcast_to(row, eye.shape), 0.0), axis=1, keepdims=True)


def store_payload(ref, outs, lse_rows):
    count = len(outs)
    for at, block in enumerate(outs):
        ref[at * 128 : (at + 1) * 128, :] = block.astype(jnp.bfloat16)
    stats = jnp.concatenate(lse_rows, axis=0)
    high = stats.astype(jnp.bfloat16)
    rest = stats - high.astype(jnp.float32)
    middle = rest.astype(jnp.bfloat16)
    low = (rest - middle.astype(jnp.float32)).astype(jnp.bfloat16)
    pieces = [p.astype(jnp.float32) for p in (high, middle, low)]
    pad = jnp.zeros((STAT_ROWS - PIECES * count, 128), jnp.float32)
    ref[count * 128 : count * 128 + STAT_ROWS, :] = jnp.concatenate(pieces + [pad], axis=0).astype(
        jnp.bfloat16
    )


def attention_kernel(scal_ref, q_ref, nk_ref, nv_ref, *refs, sources, chunk, group_size, with_new):
    out_ref, q_buf, s_buf, max_buf, sum_buf, acc_buf, k_buf, v_buf, k_sems, v_sems = refs[
        2 * sources :
    ]
    rows_in = q_ref.shape[0]
    groups = q_ref.shape[1] // (group_size * DH)
    rows = rows_in * group_size
    length = refs[0].shape[0]
    steps = length // chunk
    factor = DH ** (-0.5) * LOG2E
    first = scal_ref[sources + 1]

    def columns(j):
        return pl.ds(pl.multiple_of((first + j) * DH, DH), DH)

    def copy_of(i, c, which):
        buffer, sems = ((k_buf, k_sems), (v_buf, v_sems))[which]
        return pltpu.make_async_copy(
            refs[2 * i + which].at[
                pl.ds(c * chunk, chunk), pl.ds(pl.multiple_of(first * DH, DH), groups * DH)
            ],
            buffer.at[pl.ds(i * length + c * chunk, chunk), :],
            sems.at[i * steps + c],
        )

    for which in (0, 1):
        for i in range(sources):
            for c in range(steps):

                @pl.when(c * chunk < scal_ref[i])
                def _(i=i, c=c, which=which):
                    copy_of(i, c, which).start()

    for j in range(groups):
        base = j * group_size * DH
        q_buf[j] = jnp.concatenate(
            [q_ref[:, base + h * DH : base + (h + 1) * DH] for h in range(group_size)], axis=0
        )
    max_buf[...] = jnp.full(max_buf.shape, NEG, jnp.float32)
    sum_buf[...] = jnp.zeros(sum_buf.shape, jnp.float32)
    acc_buf[...] = jnp.zeros(acc_buf.shape, jnp.float32)
    new_scores = []
    if with_new:
        shape = (rows, nk_ref.shape[0])
        new_masks = (
            lax.broadcasted_iota(jnp.int32, shape, 1)
            <= lax.broadcasted_iota(jnp.int32, shape, 0) % rows_in + scal_ref[sources]
        )
        for j in range(groups):
            fresh = lax.dot_general(
                q_buf[j],
                nk_ref[:, columns(j)],
                (((1,), (1,)), ((), ())),
                preferred_element_type=jnp.float32,
            )
            new_scores.append(jnp.where(new_masks, fresh, NEG))

    def wait_for(u, which):
        buffer, sems = ((k_buf, k_sems), (v_buf, v_sems))[which]
        pltpu.make_async_copy(
            refs[which].at[pl.ds(0, chunk), pl.ds(pl.multiple_of(first * DH, DH), groups * DH)],
            buffer.at[pl.ds(pl.multiple_of(u * chunk, chunk), chunk), :],
            sems.at[u],
        ).wait()

    def left_of(u):
        return scal_ref[u // steps] - u % steps * chunk

    def scores_of(u, left):
        span = pl.ds(pl.multiple_of(u * chunk, chunk), chunk)
        wait_for(u, 0)
        for j in range(groups):
            scores = lax.dot_general(
                q_buf[j],
                k_buf[span, j * DH : (j + 1) * DH],
                (((1,), (1,)), ((), ())),
                preferred_element_type=jnp.float32,
            )
            if left is not None:
                places = lax.broadcasted_iota(jnp.int32, scores.shape, 1)
                scores = jnp.where(places < left, scores, NEG)
            s_buf[j, :, span] = scores
            top = max_buf[j]
            for part in range(chunk // 128):
                top = jnp.maximum(top, scores[:, part * 128 : (part + 1) * 128])
            max_buf[j] = top

    def scores_step(u, carry):
        left = left_of(u)

        @pl.when(left >= chunk)
        def _():
            scores_of(u, None)

        @pl.when((left > 0) & (left < chunk))
        def _():
            scores_of(u, left)

        return carry

    lax.fori_loop(0, sources * steps, scores_step, 0)
    peaks = []
    for j in range(groups):
        peak = jnp.max(max_buf[j], axis=1, keepdims=True)
        if with_new:
            peak = jnp.maximum(peak, jnp.max(new_scores[j], axis=1, keepdims=True))
        peaks.append(peak * factor)

    def weights_step(u, carry):
        @pl.when(left_of(u) > 0)
        def _():
            span = pl.ds(pl.multiple_of(u * chunk, chunk), chunk)
            wait_for(u, 1)
            for j in range(groups):
                weights = jnp.exp2(s_buf[j, :, span] * factor - peaks[j])
                total = sum_buf[j]
                for part in range(chunk // 128):
                    total = total + weights[:, part * 128 : (part + 1) * 128]
                sum_buf[j] = total
                acc_buf[j] += jnp.dot(
                    weights.astype(jnp.bfloat16),
                    v_buf[span, j * DH : (j + 1) * DH],
                    preferred_element_type=jnp.float32,
                )

        return carry

    lax.fori_loop(0, sources * steps, weights_step, 0)
    eye = identity_mask(128)
    outs = []
    lse_rows = []
    for j in range(groups):
        total = jnp.sum(sum_buf[j], axis=1, keepdims=True)
        summed = acc_buf[j]
        if with_new:
            weights = jnp.where(new_masks, jnp.exp2(new_scores[j] * factor - peaks[j]), 0.0)
            total = total + jnp.sum(weights, axis=1, keepdims=True)
            summed = summed + jnp.dot(
                weights.astype(jnp.bfloat16),
                nv_ref[:, columns(j)],
                preferred_element_type=jnp.float32,
            )
        filled = total > 0.0
        safe = jnp.where(filled, total, 1.0)
        lse = jnp.where(filled, peaks[j] + jnp.log(safe) * LOG2E, NEG)
        result = summed / safe
        for part in range(rows // 128):
            span = slice(part * 128, (part + 1) * 128)
            outs.append(result[span])
            lse_rows.append(column_to_row(lse[span], eye))
    store_payload(out_ref, outs, lse_rows)


def merge_kernel(*refs, final, rows_in):
    parts, out_ref = refs[:-1], refs[-1]
    blocks = (parts[0].shape[0] - STAT_ROWS) // 128
    eye = identity_mask(128)
    lses = []
    for ref in parts:
        stats = ref[blocks * 128 : blocks * 128 + STAT_ROWS, :].astype(jnp.float32)
        lse = stats[0:blocks]
        for piece in range(1, PIECES):
            lse = lse + stats[piece * blocks : (piece + 1) * blocks]
        lses.append(lse)
    peak = lses[0]
    for lse in lses[1:]:
        peak = jnp.maximum(peak, lse)
    shares = [jnp.exp2(lse - peak) for lse in lses]
    total = shares[0]
    for share in shares[1:]:
        total = total + share
    outs = []
    for at in range(blocks):
        mixed = None
        for ref, share in zip(parts, shares):
            scale = row_to_column((share / total)[at : at + 1], eye)
            term = ref[at * 128 : (at + 1) * 128, :].astype(jnp.float32) * scale
            mixed = term if mixed is None else mixed + term
        outs.append(mixed)
    if not final:
        merged = peak + jnp.log(total) * LOG2E
        store_payload(out_ref, outs, [merged[at : at + 1] for at in range(blocks)])
        return
    heads_in = 128 // rows_in
    for at in range(blocks):
        for h in range(heads_in):
            head = at * heads_in + h
            out_ref[:, head * DH : (head + 1) * DH] = outs[at][
                h * rows_in : (h + 1) * rows_in
            ].astype(jnp.bfloat16)


def gather_rows(scal_ref, mine, other, left_buf):
    core = scal_ref[0]
    rows, half = mine[0].shape
    for s in range(len(mine)):
        at = pl.multiple_of(scal_ref[1 + s] * rows, rows)
        left_buf[pl.ds(at, rows), pl.ds(pl.multiple_of(core * half, half), half)] = mine[s][...]
        left_buf[pl.ds(at, rows), pl.ds(pl.multiple_of((1 - core) * half, half), half)] = other[s][
            ...
        ]


def projection_kernel(scal_ref, *refs, devices, start):
    mine, other = refs[:devices], refs[devices : 2 * devices]
    weight_ref, out_ref, left_buf = refs[2 * devices :]
    gather_rows(scal_ref, mine, other, left_buf)
    out_ref[...] = jnp.dot(
        left_buf[...],
        weight_ref[:, start : start + out_ref.shape[1]],
        preferred_element_type=jnp.float32,
    ).astype(jnp.bfloat16)


def prepare_kernel(scal_ref, residual_ref, gain_ref, *refs, parts):
    own, other = refs[:parts], refs[parts : 2 * parts]
    hidden_ref, left_ref, squares_ref = refs[2 * parts :]
    core = scal_ref[0]
    rows, width = residual_ref.shape
    half = rows // 2
    sums = [
        a[...].astype(jnp.float32) + b[...].astype(jnp.float32) for a, b in zip(own, other)
    ]
    values = residual_ref[...].astype(jnp.float32) + jnp.concatenate(sums, axis=1)
    hidden = values.astype(jnp.bfloat16)
    hidden_ref[...] = hidden
    values = hidden.astype(jnp.float32)
    squares = jnp.sum(values * values, axis=1, keepdims=True)
    squares_ref[...] = jnp.broadcast_to(column_to_row(squares, identity_mask(rows)), squares_ref.shape)
    gained = (values * gain_ref[...]).astype(jnp.bfloat16)
    low, high = gained[:half], gained[half:]
    keep = jnp.where(core == 0, low, high)
    send = jnp.where(core == 0, high, low)
    places = lax.broadcasted_iota(jnp.int32, (128, 256), 0) * 2
    spots = lax.broadcasted_iota(jnp.int32, (128, 256), 1)
    spread = [jnp.where(spots == places + s, 1.0, 0.0).astype(jnp.bfloat16) for s in (0, 1)]
    for k in range(width // 128):
        for at, source in ((0, keep), (2, send)):
            for s in (0, 1):
                left_ref[(at + s) * half : (at + s + 1) * half, k * 256 : (k + 1) * 256] = jnp.dot(
                    source[:, k * 128 : (k + 1) * 128], spread[s], preferred_element_type=jnp.float32
                ).astype(jnp.bfloat16)


def gate_up_kernel(left_ref, weight_ref, keep_ref, send_ref):
    rows = keep_ref.shape[0]
    depth, two, width = weight_ref.shape
    merged_weight = weight_ref.reshape(depth * two, width)[...]
    both = jnp.dot(left_ref[...], merged_weight, preferred_element_type=jnp.float32)
    keep_ref[...] = both[:rows].astype(jnp.bfloat16)
    send_ref[...] = both[rows:].astype(jnp.bfloat16)


def activation_kernel(scal_ref, own_ref, other_ref, squares_ref, out_ref):
    core = scal_ref[0]
    half = out_ref.shape[0]
    total = 2 * half
    both = own_ref[...].astype(jnp.float32) + other_ref[...].astype(jnp.float32)
    factor = lax.rsqrt(squares_ref[0:1, :] / D + EPSILON)
    column = row_to_column(factor, identity_mask(total))
    column = jnp.where(core == 0, column[:half], column[half:])
    gate = both[:half] * column
    up = both[half:] * column
    out_ref[...] = (gate / (1.0 + jnp.exp(-gate)) * up).astype(jnp.bfloat16)


def down_kernel(scal_ref, *refs, pieces, last):
    mine, other = refs[:pieces], refs[pieces : 2 * pieces]
    rest = refs[2 * pieces :]
    core = scal_ref[0]
    half, part = mine[0].shape
    if last:
        before_ref, weight_ref, keep_ref, send_ref, left_buf, out_buf = rest
    else:
        weight_ref, out_ref, left_buf = rest
    for s in range(pieces):
        span = pl.ds(pl.multiple_of(scal_ref[2 + s] * part, part), part)
        left_buf[pl.ds(pl.multiple_of(core * half, half), half), span] = mine[s][...]
        left_buf[pl.ds(pl.multiple_of((1 - core) * half, half), half), span] = other[s][...]
    product = jnp.dot(left_buf[...], weight_ref[...], preferred_element_type=jnp.float32)
    if not last:
        out_ref[...] = product
        return
    side = scal_ref[1]
    out_buf[...] = before_ref[...] + product
    keep_ref[...] = out_buf[pl.ds(pl.multiple_of(side * half, half), half), :]
    send_ref[...] = out_buf[pl.ds(pl.multiple_of((1 - side) * half, half), half), :].astype(
        jnp.bfloat16
    )


def load_kernel(source_ref, out_ref, sems, *, start):
    size = out_ref.shape[0] // LANES
    copies = [
        pltpu.make_async_copy(
            source_ref.at[pl.ds(start + i * size, size), :],
            out_ref.at[pl.ds(i * size, size), :],
            sems.at[i],
        )
        for i in range(LANES)
    ]
    for copy in copies:
        copy.start()
    for copy in copies:
        copy.wait()


def loaded(weight, start, count):
    return pl.pallas_call(
        functools.partial(load_kernel, start=start),
        out_shape=jax.ShapeDtypeStruct((count, weight.shape[1]), weight.dtype),
        in_specs=[far()],
        out_specs=vmem(),
        scratch_shapes=[pltpu.SemaphoreType.DMA((LANES,))],
        compiler_params=pltpu.CompilerParams(vmem_limit_bytes=LOADING),
        cost_estimate=cost(0, 4 * count * weight.shape[1]),
        name="load",
    )(weight)


def vmem():
    return pl.BlockSpec(memory_space=pltpu.VMEM)


def far():
    return pl.BlockSpec(memory_space=pltpu.HBM)


def smem():
    return pl.BlockSpec(memory_space=pltpu.SMEM)


def cost(flops, size):
    return pl.CostEstimate(flops=int(flops), bytes_accessed=int(size), transcendentals=0)


def attend_block(scal, with_new, queries, sources, new_keys, new_values, group_size):
    length, width = sources[0][0].shape
    rows_in = queries.shape[0]
    groups = width // DH // 2
    rows = rows_in * group_size
    chunk = next(c for c in (1536, 1024, 512, 256, 128) if length % c == 0)
    keys = len(sources) * length
    return pl.pallas_call(
        functools.partial(
            attention_kernel,
            sources=len(sources),
            chunk=chunk,
            group_size=group_size,
            with_new=with_new,
        ),
        out_shape=jax.ShapeDtypeStruct((groups * rows + STAT_ROWS, DH), jnp.bfloat16),
        in_specs=[smem()] + [vmem()] * 3 + [far()] * (2 * len(sources)),
        out_specs=vmem(),
        scratch_shapes=[
            pltpu.VMEM((groups, rows, DH), jnp.bfloat16),
            pltpu.VMEM((groups, rows, keys), jnp.float32),
            pltpu.VMEM((groups, rows, 128), jnp.float32),
            pltpu.VMEM((groups, rows, 128), jnp.float32),
            pltpu.VMEM((groups, rows, DH), jnp.float32),
            pltpu.VMEM((keys, groups * DH), jnp.bfloat16),
            pltpu.VMEM((keys, groups * DH), jnp.bfloat16),
            pltpu.SemaphoreType.DMA((keys // chunk,)),
            pltpu.SemaphoreType.DMA((keys // chunk,)),
        ],
        compiler_params=pltpu.CompilerParams(vmem_limit_bytes=ALONE if with_new and len(sources) == 1 else LARGE),
        cost_estimate=cost(4 * groups * rows * keys * DH * 3, 4 * keys * width),
        name="attend",
    )(scal, queries, new_keys, new_values, *[a for pair in sources for a in pair])


def merged(parts, final, rows_in):
    blocks = (parts[0].shape[0] - STAT_ROWS) // 128
    if final:
        shape = (rows_in, blocks * 128 // rows_in * DH)
    else:
        shape = parts[0].shape
    return pl.pallas_call(
        functools.partial(merge_kernel, final=final, rows_in=rows_in),
        out_shape=jax.ShapeDtypeStruct(shape, jnp.bfloat16),
        in_specs=[vmem()] * len(parts),
        out_specs=vmem(),
        cost_estimate=cost(blocks * 128 * 128 * 8 * len(parts), parts[0].size * 2 * len(parts)),
        compiler_params=pltpu.CompilerParams(vmem_limit_bytes=SMALL),
        name="merge",
    )(*parts)


def project(scal, mine, other, weight, start, count):
    devices = len(mine)
    rows = mine[0].shape[0] * devices
    depth = weight.shape[0]
    return pl.pallas_call(
        functools.partial(projection_kernel, devices=devices, start=start),
        out_shape=jax.ShapeDtypeStruct((rows, count), jnp.bfloat16),
        in_specs=[smem()] + [vmem()] * (2 * devices + 1),
        out_specs=vmem(),
        scratch_shapes=[pltpu.VMEM((rows, depth), jnp.bfloat16)],
        compiler_params=pltpu.CompilerParams(vmem_limit_bytes=MEDIUM),
        cost_estimate=cost(2 * rows * depth * count, 2 * depth * count),
        name="project",
    )(scal, *mine, *other, weight)


def prepare(scal, residual, gain, own, other):
    rows, width = residual.shape
    return pl.pallas_call(
        functools.partial(prepare_kernel, parts=len(own)),
        out_shape=(
            jax.ShapeDtypeStruct((rows, width), jnp.bfloat16),
            jax.ShapeDtypeStruct((2 * rows, 2 * width), jnp.bfloat16),
            jax.ShapeDtypeStruct((8, rows), jnp.float32),
        ),
        in_specs=[smem()] + [vmem()] * (2 + 2 * len(own)),
        out_specs=(vmem(),) * 3,
        cost_estimate=cost(rows * width * 1024, rows * width * 8),
        compiler_params=pltpu.CompilerParams(vmem_limit_bytes=SMALL),
        name="prepare",
    )(scal, residual, gain.reshape(1, width), *own, *other)


def gate_up_part(left, weight, start, count, tile):
    rows2, depth2 = left.shape
    depth = depth2 // 2
    rows = rows2 // 2
    first = start // tile
    out = jax.ShapeDtypeStruct((rows, count), jnp.bfloat16)
    return pl.pallas_call(
        gate_up_kernel,
        grid=(count // tile,),
        out_shape=(out, out),
        in_specs=[
            pl.BlockSpec((rows2, depth2), lambda i: (0, 0)),
            pl.BlockSpec((depth, 2, tile), lambda i: (0, 0, first + i)),
        ],
        out_specs=(
            pl.BlockSpec((rows, tile), lambda i: (0, i)),
            pl.BlockSpec((rows, tile), lambda i: (0, i)),
        ),
        compiler_params=pltpu.CompilerParams(vmem_limit_bytes=LARGE),
        cost_estimate=cost(2 * rows2 * depth2 * count, 4 * depth * count),
        name="gate_up",
    )(left, weight)


def activate(scal, own, other, squares):
    rows, width = own.shape
    return pl.pallas_call(
        activation_kernel,
        out_shape=jax.ShapeDtypeStruct((rows // 2, width), jnp.bfloat16),
        in_specs=[smem()] + [vmem()] * 3,
        out_specs=vmem(),
        cost_estimate=cost(rows * width * 16, rows * width * 5),
        compiler_params=pltpu.CompilerParams(vmem_limit_bytes=SMALL),
        name="activate",
    )(scal, own, other, squares)


def down_project(scal, mine, other, weight, before):
    pieces = len(mine)
    half, _ = mine[0].shape
    depth, width = weight.shape
    last = before is not None
    inputs = [*mine, *other] + ([before] if last else [])
    scratch = [pltpu.VMEM((2 * half, depth), jnp.bfloat16)]
    if last:
        out_shape = (
            jax.ShapeDtypeStruct((half, width), jnp.float32),
            jax.ShapeDtypeStruct((half, width), jnp.bfloat16),
        )
        out_specs = (vmem(), vmem())
        scratch.append(pltpu.VMEM((2 * half, width), jnp.float32))
    else:
        out_shape = jax.ShapeDtypeStruct((2 * half, width), jnp.float32)
        out_specs = vmem()
    return pl.pallas_call(
        functools.partial(down_kernel, pieces=pieces, last=last),
        in_specs=[smem()] + [vmem()] * (len(inputs) + 1),
        out_specs=out_specs,
        scratch_shapes=scratch,
        out_shape=out_shape,
        compiler_params=pltpu.CompilerParams(vmem_limit_bytes=MEDIUM),
        cost_estimate=cost(4 * half * depth * width, 2 * depth * width),
        name="down",
    )(scal, *inputs, weight)


def fold_kernel(scal_ref, own_ref, come_ref, away_ref, keep_ref):
    upper = scal_ref[0]
    width = keep_ref.shape[1]
    for out_ref, which in ((away_ref, 1 - upper), (keep_ref, upper)):
        span = pl.ds(pl.multiple_of(which * width, 128), width)
        out_ref[...] = (
            own_ref[:, span].astype(jnp.float32) + come_ref[:, span].astype(jnp.float32)
        ).astype(jnp.bfloat16)


def fold(scal, own, come):
    rows, width = own.shape
    out = jax.ShapeDtypeStruct((rows, width // 2), jnp.bfloat16)
    return pl.pallas_call(
        fold_kernel,
        out_shape=(out, out),
        in_specs=[smem()] + [vmem()] * 2,
        out_specs=(vmem(), vmem()),
        compiler_params=pltpu.CompilerParams(vmem_limit_bytes=SMALL),
        cost_estimate=cost(rows * width, rows * width * 6),
        name="fold",
    )(scal, own, come)


def half_of(value, which, axis=1):
    size = value.shape[axis] // 2
    return lax.dynamic_slice_in_dim(value, which * size, size, axis)


def on_device_line(
    queries,
    cache_keys,
    cache_values,
    new_keys,
    new_values,
    cache_blocks,
    residual,
    norm_gain,
    out_weight,
    gate_up,
    down_weight,
):
    devices = lax.axis_size("ctx")
    place = lax.axis_index("ctx")
    core = lax.axis_index("khalf")
    side = lax.axis_index("kv")
    group_size = HQ // KVH
    rows_in = queries.shape[0]
    length = cache_keys.shape[0]
    mine_valid, other_valid = (
        jnp.clip(cache_blocks[0] * BLOCK - (place * 2 + c) * length, 0, length)
        for c in (core, 1 - core)
    )
    bits = [1 << b for b in range(devices.bit_length() - 1)]
    sources = [(place - s) % devices for s in range(devices)]
    blocks = [
        sum((source // bit) % 2 * (devices // (2 * bit)) for bit in bits) for source in sources
    ]
    groups = cache_keys.shape[1] // DH // 2
    offsets = [(source - place) * rows_in for source in sources]

    def packed(*values):
        return jnp.stack(values).astype(jnp.int32)

    early = (
        half_of(queries, core),
        packed(mine_valid, 0, core * groups),
        packed(other_valid, 0, core * groups),
        [packed(mine_valid, other_valid, o, core * groups) for o in offsets[1:]],
        packed(core, *sources),
        packed(core, side),
        packed(core, side, *blocks),
        [packed((place // bit) % 2) for bit in bits],
    )
    early = lax.optimization_barrier(early)
    q_mine, own_scal, rest_scal, visit_scals, source_scal, core_scal, down_scal, bit_scals = early
    order = sorted(range(1, devices), key=lambda s: min(s, devices - s))
    visiting = {}
    for s in order:
        visiting[s] = rotation(q_mine, "ctx", s)
    k_there = exchanged(cache_keys, "khalf", 1)
    v_there = exchanged(cache_values, "khalf", 1)
    here, there = (cache_keys, cache_values), (k_there, v_there)
    last = attend_block(
        own_scal, True, q_mine, [here], new_keys, new_values, group_size
    )
    parts = [last]
    for s in order:
        visitor, last = lax.optimization_barrier((visiting[s], last))
        last = attend_block(
            visit_scals[s - 1],
            True,
            visitor,
            [here, there],
            new_keys,
            new_values,
            group_size,
        )
        parts.append(rotation(last, "ctx", -s))
    q_mine, last = lax.optimization_barrier((q_mine, last))
    parts.append(attend_block(rest_scal, False, q_mine, [there], new_keys, new_values, group_size))
    attention = merged(parts, True, rows_in)
    mine = [attention]
    for s in range(1, devices):
        mine.append(rotation(attention, "ctx", s))
    other = [exchanged(a, "khalf", 1) for a in mine]
    out_near = loaded(out_weight, 0, out_weight.shape[0])
    own, come = [], []
    width = out_weight.shape[1] // SLABS
    for slab in range(SLABS):
        own.append(project(source_scal, mine, other, out_near, slab * width, width))
        come.append(exchanged(own[-1], "kv", 1))
    hidden, left, squares = prepare(core_scal, residual, norm_gain, own, come)
    for bit in bits:
        squares = squares + exchanged(squares, "ctx", bit)
    squares = squares + exchanged(squares, "khalf", 1)
    unit = gate_up.shape[2] // sum(STREAMS)
    starts = [unit * sum(STREAMS[:i]) for i in range(len(STREAMS))]
    spans = [unit * share for share in STREAMS]
    down = None
    down_near = []
    for start, span in zip(starts, spans):
        down_near.append(loaded(down_weight, start, span))
    for stream, (start, span) in enumerate(zip(starts, spans)):
        keep, send = gate_up_part(left, gate_up, start, span, unit)
        come = exchanged(send, "khalf", 1)
        for bit, bit_scal in zip(bits, bit_scals):
            away, keep = fold(bit_scal, keep, come)
            if bit == 1:
                away, left = lax.optimization_barrier((away, left))
            come = exchanged(away, "ctx", bit)
        activated = activate(core_scal, keep, come, squares)
        mine, other = [], []
        for s in range(devices):
            piece = activated
            if s:
                piece = rotation(activated, "ctx", s)
            mine.append(piece)
            other.append(exchanged(piece, "khalf", 1))
        down = down_project(down_scal, mine, other, down_near[stream], down)
    keep, send = down
    come = exchanged(send, "kv", 1)
    kept = half_of(hidden, side, 0)
    return (kept.astype(jnp.float32) + keep + come.astype(jnp.float32)).astype(jnp.bfloat16)


def line_fits(mesh, keys_shape, hidden_width):
    sizes = dict(mesh.shape)
    ctx, kv, khalf = sizes["ctx"], sizes["kv"], sizes["khalf"]
    groups = keys_shape[1] // kv // DH
    length = keys_shape[0] // (sizes["groups"] * ctx * khalf)
    return (
        ctx & (ctx - 1) == 0
        and kv == 2
        and khalf == 2
        and groups % 2 == 0
        and length % 128 == 0
        and hidden_width // kv % (sum(STREAMS) * ctx * 128) == 0
    )


def solution(mesh):
    def on_device(*arguments):
        keys, gate_up = arguments[1], arguments[9]
        sizes = dict(mesh.shape)
        keys_shape = (
            keys.shape[0] * sizes["groups"] * sizes["ctx"] * sizes["khalf"],
            keys.shape[1] * sizes["kv"],
        )
        if line_fits(mesh, keys_shape, gate_up.shape[2] * sizes["kv"]):
            return on_device_line(*arguments)
        return on_device_any(*arguments)

    in_specs = (
        P(("groups", "ctx"), "kv"),
        P(("groups", "ctx", "khalf"), "kv"),
        P(("groups", "ctx", "khalf"), "kv"),
        P(("groups", "ctx"), "kv"),
        P(("groups", "ctx"), "kv"),
        P("groups"),
        P("groups", ("ctx", "khalf")),
        P(("ctx", "khalf")),
        P("kv", ("ctx", "khalf")),
        P(("ctx", "khalf"), None, "kv"),
        P("kv", ("ctx", "khalf")),
    )
    out_specs = P(("groups", "kv"), ("ctx", "khalf"))
    return jax.shard_map(
        on_device, mesh=mesh, in_specs=in_specs, out_specs=out_specs, check_vma=False
    )
```

```python
import functools

import jax
import jax.numpy as jnp
from jax import lax
from jax.experimental import pallas as pl
from jax.experimental.pallas import tpu as pltpu
from jax.sharding import PartitionSpec as P


D = 8192
HQ = 64
KVH = 8
DH = 128
BLOCK = 128


NEG = -1e30
EPSILON = 1e-05
STREAMS = (2, 3, 2)
SLABS = 2


def shifted(value, axis, by):
    devices = lax.axis_size(axis)
    return lax.ppermute(value, axis, [(i, (i + by) % devices) for i in range(devices)])


def merged_2(value, axis, combine):
    everything = jax.tree.map(
        lambda part, kind: lax.all_gather(part.astype(kind), axis),
        value,
        jax.tree.map(lambda a: jnp.bfloat16 if a.dtype == jnp.float32 else a.dtype, value),
    )

    def take(k):
        return jax.tree.map(lambda part, own: part[k].astype(own.dtype), everything, value)

    return lax.fori_loop(
        1, lax.axis_size(axis), lambda k, so_far: combine(so_far, take(k)), take(0)
    )


def attend(query_block, key_block, value_block, allowed):
    _, local_groups, _, head_width = query_block.shape
    key_count = key_block.shape[0]
    keyed = key_block.reshape(key_count, local_groups, head_width)
    valued = value_block.reshape(key_count, local_groups, head_width)
    scores = jnp.einsum(
        "rkgd,nkd->rkgn", query_block, keyed, preferred_element_type=jnp.float32
    ) * head_width ** (-0.5)
    usable = allowed[:, None, None, :]
    scores = jnp.where(usable, scores, NEG)
    peak_score = jnp.max(scores, axis=3)
    weights = jnp.where(usable, jnp.exp(scores - peak_score[..., None]), 0.0)
    weight_sum = jnp.sum(weights, axis=3)
    summed = jnp.einsum(
        "rkgn,nkd->rkgd", weights.astype(jnp.bfloat16), valued, preferred_element_type=jnp.float32
    )
    return (summed, peak_score, weight_sum)


def combine(earlier_part, later_part):
    earlier_sum, earlier_peak, earlier_total = earlier_part
    later_sum, later_peak, later_total = later_part
    new_peak = jnp.maximum(earlier_peak, later_peak)
    earlier_scale = jnp.exp(earlier_peak - new_peak)
    later_scale = jnp.exp(later_peak - new_peak)
    return (
        earlier_sum * earlier_scale[..., None] + later_sum * later_scale[..., None],
        new_peak,
        earlier_total * earlier_scale + later_total * later_scale,
    )


def normalize(hidden_state, norm_gain):
    values32 = hidden_state.astype(jnp.float32)
    squares = lax.psum(jnp.sum(values32 * values32, axis=1), ("ctx", "khalf"))
    factor = lax.rsqrt(squares / D + EPSILON)
    return (values32 * factor[:, None] * norm_gain).astype(jnp.bfloat16)


def on_device_any(
    queries,
    cache_keys,
    cache_values,
    new_keys,
    new_values,
    cache_blocks,
    residual,
    norm_gain,
    out_weight,
    gate_up,
    down_weight,
):
    query_rows = queries.shape[0]
    group_size = HQ // KVH
    local_groups = cache_keys.shape[1] // DH
    local_queries = queries.reshape(query_rows, local_groups, group_size, DH)
    cache_length = cache_keys.shape[0]
    shard_index = lax.axis_index("ctx") * lax.axis_size("khalf") + lax.axis_index("khalf")
    positions = shard_index * cache_length + jnp.arange(cache_length, dtype=jnp.int32)
    cache_allowed = (positions < cache_blocks[0] * BLOCK)[None, :]
    query_start = lax.axis_index("ctx") * query_rows
    query_positions = query_start + jnp.arange(query_rows, dtype=jnp.int32)
    empty = (
        jnp.zeros((query_rows, local_groups, group_size, DH), jnp.float32),
        jnp.full((query_rows, local_groups, group_size), NEG, jnp.float32),
        jnp.zeros((query_rows, local_groups, group_size), jnp.float32),
    )

    def cycle_step(step_index, state_carry):
        visiting, partial_state = state_carry
        fresh = attend(visiting, cache_keys, cache_values, cache_allowed)
        partial_state = combine(partial_state, fresh)
        visiting = shifted(visiting, "ctx", 1)
        partial_state = (
            shifted(partial_state[0].astype(jnp.bfloat16), "ctx", 1).astype(jnp.float32),
            shifted(partial_state[1].astype(jnp.bfloat16), "ctx", 1).astype(jnp.float32),
            shifted(partial_state[2].astype(jnp.bfloat16), "ctx", 1).astype(jnp.float32),
        )
        return (visiting, partial_state)

    _, cache_part = lax.fori_loop(0, lax.axis_size("ctx"), cycle_step, (local_queries, empty))
    merged = merged_2(cache_part, "khalf", combine)
    piece_keys = lax.all_gather(new_keys, "ctx", axis=0, tiled=True)
    piece_values = lax.all_gather(new_values, "ctx", axis=0, tiled=True)
    key_positions = jnp.arange(piece_keys.shape[0], dtype=jnp.int32)
    allowed = key_positions[None, :] <= query_positions[:, None]
    own_part = combine(empty, attend(local_queries, piece_keys, piece_values, allowed))
    joined = combine(merged, own_part)
    attention = (
        (joined[0] / joined[2][..., None])
        .astype(jnp.bfloat16)
        .reshape(query_rows, local_groups * group_size * DH)
    )
    partial_rows = jnp.dot(
        lax.all_gather(attention, "ctx", axis=0, tiled=True),
        out_weight,
        preferred_element_type=jnp.float32,
    )
    projected = lax.psum(partial_rows.astype(jnp.bfloat16), "kv").astype(jnp.float32)
    hidden_state = (residual.astype(jnp.float32) + projected).astype(jnp.bfloat16)
    normed = normalize(hidden_state, norm_gain)
    own_rows = hidden_state.shape[0] // lax.axis_size("kv")
    kept = lax.dynamic_slice_in_dim(hidden_state, lax.axis_index("kv") * own_rows, own_rows, 0)
    local_width = gate_up.shape[0]
    local_hidden = gate_up.shape[2]
    merged_weight = gate_up.reshape(local_width, 2 * local_hidden)
    both = lax.psum_scatter(
        jnp.dot(normed, merged_weight, preferred_element_type=jnp.float32).astype(jnp.bfloat16),
        ("ctx", "khalf"),
        scatter_dimension=0,
        tiled=True,
    ).astype(jnp.float32)
    activated = (jax.nn.silu(both[:, :local_hidden]) * both[:, local_hidden:]).astype(jnp.bfloat16)
    partial_out = jnp.dot(
        lax.all_gather(activated, ("ctx", "khalf"), axis=0, tiled=True),
        down_weight,
        preferred_element_type=jnp.float32,
    )
    down = lax.psum_scatter(
        partial_out.astype(jnp.bfloat16), "kv", scatter_dimension=0, tiled=True
    ).astype(jnp.float32)
    return (kept.astype(jnp.float32) + down).astype(jnp.bfloat16)


LOG2E = 1.4426950408889634
PIECES = 3
STAT_ROWS = 16
MOST_KEYS = 4096
SMALL = 8 * 2**20
MEDIUM = 16 * 2**20
LARGE = 28 * 2**20
LOADING = 12 * 2**20
LANES = 4


def rotated(value, axis, by):
    devices = lax.axis_size(axis)
    return lax.ppermute(value, axis, [(i, (i + by) % devices) for i in range(devices)])


def exchanged(value, axis, bit):
    devices = lax.axis_size(axis)
    return lax.ppermute(value, axis, [(i, i ^ bit) for i in range(devices)])


def identity_mask(size):
    rows = lax.broadcasted_iota(jnp.int32, (size, size), 0)
    columns = lax.broadcasted_iota(jnp.int32, (size, size), 1)
    return rows == columns


def column_to_row(column, eye):
    return jnp.sum(jnp.where(eye, jnp.broadcast_to(column, eye.shape), 0.0), axis=0, keepdims=True)


def row_to_column(row, eye):
    return jnp.sum(jnp.where(eye, jnp.broadcast_to(row, eye.shape), 0.0), axis=1, keepdims=True)


def store_payload(ref, outs, lse_rows):
    count = len(outs)
    for at, block in enumerate(outs):
        ref[at * 128 : (at + 1) * 128, :] = block.astype(jnp.bfloat16)
    stats = jnp.concatenate(lse_rows, axis=0)
    high = stats.astype(jnp.bfloat16)
    rest = stats - high.astype(jnp.float32)
    middle = rest.astype(jnp.bfloat16)
    low = (rest - middle.astype(jnp.float32)).astype(jnp.bfloat16)
    pieces = [p.astype(jnp.float32) for p in (high, middle, low)]
    pad = jnp.zeros((STAT_ROWS - PIECES * count, 128), jnp.float32)
    ref[count * 128 : count * 128 + STAT_ROWS, :] = jnp.concatenate(pieces + [pad], axis=0).astype(
        jnp.bfloat16
    )


def attention_kernel(scal_ref, q_ref, nk_ref, nv_ref, *refs, sources, chunk, group_size):
    out_ref, q_buf, s_buf, max_buf, sum_buf, acc_buf, k_buf, v_buf, k_sems, v_sems = refs[
        2 * sources :
    ]
    rows_in = q_ref.shape[0]
    groups = q_ref.shape[1] // (group_size * DH)
    rows = rows_in * group_size
    length = refs[0].shape[0]
    steps = length // chunk
    factor = DH ** (-0.5) * LOG2E
    first = scal_ref[sources + 1]

    def copy_of(i, c, which):
        buffer, sems = ((k_buf, k_sems), (v_buf, v_sems))[which]
        return pltpu.make_async_copy(
            refs[2 * i + which].at[
                pl.ds(c * chunk, chunk), pl.ds(pl.multiple_of(first * DH, DH), groups * DH)
            ],
            buffer.at[pl.ds(i * length + c * chunk, chunk), :],
            sems.at[i * steps + c],
        )

    for which in (0, 1):
        for i in range(sources):
            for c in range(steps):

                @pl.when(c * chunk < scal_ref[i])
                def _(i=i, c=c, which=which):
                    copy_of(i, c, which).start()

    for j in range(groups):
        base = j * group_size * DH
        q_buf[j] = jnp.concatenate(
            [q_ref[:, base + h * DH : base + (h + 1) * DH] for h in range(group_size)], axis=0
        )
    max_buf[...] = jnp.full(max_buf.shape, NEG, jnp.float32)
    sum_buf[...] = jnp.zeros(sum_buf.shape, jnp.float32)
    acc_buf[...] = jnp.zeros(acc_buf.shape, jnp.float32)
    new_scores = []
    shape = (rows, nk_ref.shape[0])
    new_masks = (
        lax.broadcasted_iota(jnp.int32, shape, 1)
        <= lax.broadcasted_iota(jnp.int32, shape, 0) % rows_in + scal_ref[sources]
    )
    for j in range(groups):
        fresh = lax.dot_general(
            q_buf[j],
            nk_ref[:, j * DH : (j + 1) * DH],
            (((1,), (1,)), ((), ())),
            preferred_element_type=jnp.float32,
        )
        new_scores.append(jnp.where(new_masks, fresh, NEG))

    def wait_for(u, which):
        buffer, sems = ((k_buf, k_sems), (v_buf, v_sems))[which]
        pltpu.make_async_copy(
            refs[which].at[pl.ds(0, chunk), pl.ds(pl.multiple_of(first * DH, DH), groups * DH)],
            buffer.at[pl.ds(pl.multiple_of(u * chunk, chunk), chunk), :],
            sems.at[u],
        ).wait()

    def left_of(u):
        return scal_ref[u // steps] - u % steps * chunk

    def scores_of(u, left):
        span = pl.ds(pl.multiple_of(u * chunk, chunk), chunk)
        wait_for(u, 0)
        for j in range(groups):
            scores = lax.dot_general(
                q_buf[j],
                k_buf[span, j * DH : (j + 1) * DH],
                (((1,), (1,)), ((), ())),
                preferred_element_type=jnp.float32,
            )
            if left is not None:
                places = lax.broadcasted_iota(jnp.int32, scores.shape, 1)
                scores = jnp.where(places < left, scores, NEG)
            s_buf[j, :, span] = scores
            top = max_buf[j]
            for part in range(chunk // 128):
                top = jnp.maximum(top, scores[:, part * 128 : (part + 1) * 128])
            max_buf[j] = top

    def scores_step(u, carry):
        left = left_of(u)

        @pl.when(left >= chunk)
        def _():
            scores_of(u, None)

        @pl.when((left > 0) & (left < chunk))
        def _():
            scores_of(u, left)

        return carry

    lax.fori_loop(0, sources * steps, scores_step, 0)
    peaks = []
    for j in range(groups):
        peak = jnp.max(max_buf[j], axis=1, keepdims=True)
        peak = jnp.maximum(peak, jnp.max(new_scores[j], axis=1, keepdims=True))
        peaks.append(peak * factor)

    def weights_step(u, carry):
        @pl.when(left_of(u) > 0)
        def _():
            span = pl.ds(pl.multiple_of(u * chunk, chunk), chunk)
            wait_for(u, 1)
            for j in range(groups):
                weights = jnp.exp2(s_buf[j, :, span] * factor - peaks[j])
                total = sum_buf[j]
                for part in range(chunk // 128):
                    total = total + weights[:, part * 128 : (part + 1) * 128]
                sum_buf[j] = total
                acc_buf[j] += jnp.dot(
                    weights.astype(jnp.bfloat16),
                    v_buf[span, j * DH : (j + 1) * DH],
                    preferred_element_type=jnp.float32,
                )

        return carry

    lax.fori_loop(0, sources * steps, weights_step, 0)
    eye = identity_mask(128)
    outs = []
    lse_rows = []
    for j in range(groups):
        total = jnp.sum(sum_buf[j], axis=1, keepdims=True)
        summed = acc_buf[j]
        weights = jnp.where(new_masks, jnp.exp2(new_scores[j] * factor - peaks[j]), 0.0)
        total = total + jnp.sum(weights, axis=1, keepdims=True)
        summed = summed + jnp.dot(
            weights.astype(jnp.bfloat16),
            nv_ref[:, j * DH : (j + 1) * DH],
            preferred_element_type=jnp.float32,
        )
        filled = total > 0.0
        safe = jnp.where(filled, total, 1.0)
        lse = jnp.where(filled, peaks[j] + jnp.log(safe) * LOG2E, NEG)
        result = summed / safe
        for part in range(rows // 128):
            span = slice(part * 128, (part + 1) * 128)
            outs.append(result[span])
            lse_rows.append(column_to_row(lse[span], eye))
    store_payload(out_ref, outs, lse_rows)


def merge_kernel(*refs, final, rows_in):
    parts, out_ref = refs[:-1], refs[-1]
    blocks = (parts[0].shape[0] - STAT_ROWS) // 128
    eye = identity_mask(128)
    lses = []
    for ref in parts:
        stats = ref[blocks * 128 : blocks * 128 + STAT_ROWS, :].astype(jnp.float32)
        lse = stats[0:blocks]
        for piece in range(1, PIECES):
            lse = lse + stats[piece * blocks : (piece + 1) * blocks]
        lses.append(lse)
    peak = lses[0]
    for lse in lses[1:]:
        peak = jnp.maximum(peak, lse)
    shares = [jnp.exp2(lse - peak) for lse in lses]
    total = shares[0]
    for share in shares[1:]:
        total = total + share
    outs = []
    for at in range(blocks):
        mixed = None
        for ref, share in zip(parts, shares):
            scale = row_to_column((share / total)[at : at + 1], eye)
            term = ref[at * 128 : (at + 1) * 128, :].astype(jnp.float32) * scale
            mixed = term if mixed is None else mixed + term
        outs.append(mixed)
    if not final:
        merged = peak + jnp.log(total) * LOG2E
        store_payload(out_ref, outs, [merged[at : at + 1] for at in range(blocks)])
        return
    heads_in = 128 // rows_in
    for at in range(blocks):
        for h in range(heads_in):
            head = at * heads_in + h
            out_ref[:, head * DH : (head + 1) * DH] = outs[at][
                h * rows_in : (h + 1) * rows_in
            ].astype(jnp.bfloat16)


def gather_rows(scal_ref, mine, other, left_buf):
    core = scal_ref[0]
    rows, half = mine[0].shape
    for s in range(len(mine)):
        at = pl.multiple_of(scal_ref[1 + s] * rows, rows)
        left_buf[pl.ds(at, rows), pl.ds(pl.multiple_of(core * half, half), half)] = mine[s][...]
        left_buf[pl.ds(at, rows), pl.ds(pl.multiple_of((1 - core) * half, half), half)] = other[s][
            ...
        ]


def projection_kernel(scal_ref, *refs, devices, start):
    mine, other = refs[:devices], refs[devices : 2 * devices]
    weight_ref, out_ref, left_buf = refs[2 * devices :]
    gather_rows(scal_ref, mine, other, left_buf)
    out_ref[...] = jnp.dot(
        left_buf[...],
        weight_ref[:, start : start + out_ref.shape[1]],
        preferred_element_type=jnp.float32,
    ).astype(jnp.bfloat16)


def prepare_kernel(scal_ref, residual_ref, gain_ref, *refs, parts):
    own, other = refs[:parts], refs[parts : 2 * parts]
    hidden_ref, left_ref, squares_ref = refs[2 * parts :]
    core = scal_ref[0]
    rows, width = residual_ref.shape
    half = rows // 2
    sums = [
        a[...].astype(jnp.float32) + b[...].astype(jnp.float32) for a, b in zip(own, other)
    ]
    values = residual_ref[...].astype(jnp.float32) + jnp.concatenate(sums, axis=1)
    hidden = values.astype(jnp.bfloat16)
    hidden_ref[...] = hidden
    values = hidden.astype(jnp.float32)
    squares = jnp.sum(values * values, axis=1, keepdims=True)
    squares_ref[...] = jnp.broadcast_to(column_to_row(squares, identity_mask(rows)), squares_ref.shape)
    gained = (values * gain_ref[...]).astype(jnp.bfloat16)
    low, high = gained[:half], gained[half:]
    keep = jnp.where(core == 0, low, high)
    send = jnp.where(core == 0, high, low)
    places = lax.broadcasted_iota(jnp.int32, (128, 256), 0) * 2
    spots = lax.broadcasted_iota(jnp.int32, (128, 256), 1)
    spread = [jnp.where(spots == places + s, 1.0, 0.0).astype(jnp.bfloat16) for s in (0, 1)]
    for k in range(width // 128):
        for at, source in ((0, keep), (2, send)):
            for s in (0, 1):
                left_ref[(at + s) * half : (at + s + 1) * half, k * 256 : (k + 1) * 256] = jnp.dot(
                    source[:, k * 128 : (k + 1) * 128], spread[s], preferred_element_type=jnp.float32
                ).astype(jnp.bfloat16)


def gate_up_kernel(left_ref, weight_ref, keep_ref, send_ref):
    rows = keep_ref.shape[0]
    depth, two, width = weight_ref.shape
    merged_weight = weight_ref.reshape(depth * two, width)[...]
    both = jnp.dot(left_ref[...], merged_weight, preferred_element_type=jnp.float32)
    keep_ref[...] = both[:rows].astype(jnp.bfloat16)
    send_ref[...] = both[rows:].astype(jnp.bfloat16)


def activation_kernel(scal_ref, own_ref, other_ref, squares_ref, out_ref):
    core = scal_ref[0]
    half = out_ref.shape[0]
    total = 2 * half
    both = own_ref[...].astype(jnp.float32) + other_ref[...].astype(jnp.float32)
    factor = lax.rsqrt(squares_ref[0:1, :] / D + EPSILON)
    column = row_to_column(factor, identity_mask(total))
    column = jnp.where(core == 0, column[:half], column[half:])
    gate = both[:half] * column
    up = both[half:] * column
    out_ref[...] = (gate / (1.0 + jnp.exp(-gate)) * up).astype(jnp.bfloat16)


def down_kernel(scal_ref, *refs, pieces, first, last):
    mine, other = refs[:pieces], refs[pieces : 2 * pieces]
    rest = refs[2 * pieces :]
    core = scal_ref[0]
    half, part = mine[0].shape
    if not first:
        before_ref, *rest = rest
    if last:
        weight_ref, keep_ref, send_ref, left_buf, out_buf = rest
    else:
        weight_ref, out_ref, left_buf = rest
    for s in range(pieces):
        span = pl.ds(pl.multiple_of(scal_ref[2 + s] * part, part), part)
        left_buf[pl.ds(pl.multiple_of(core * half, half), half), span] = mine[s][...]
        left_buf[pl.ds(pl.multiple_of((1 - core) * half, half), half), span] = other[s][...]
    product = jnp.dot(left_buf[...], weight_ref[...], preferred_element_type=jnp.float32)
    if not first:
        product = before_ref[...] + product
    if not last:
        out_ref[...] = product
        return
    side = scal_ref[1]
    out_buf[...] = product
    keep_ref[...] = out_buf[pl.ds(pl.multiple_of(side * half, half), half), :]
    send_ref[...] = out_buf[pl.ds(pl.multiple_of((1 - side) * half, half), half), :].astype(
        jnp.bfloat16
    )


def load_kernel(source_ref, out_ref, sems, *, start):
    size = out_ref.shape[0] // LANES
    copies = [
        pltpu.make_async_copy(
            source_ref.at[pl.ds(start + i * size, size), :],
            out_ref.at[pl.ds(i * size, size), :],
            sems.at[i],
        )
        for i in range(LANES)
    ]
    for copy in copies:
        copy.start()
    for copy in copies:
        copy.wait()


def loaded(weight, start, count):
    return pl.pallas_call(
        functools.partial(load_kernel, start=start),
        out_shape=jax.ShapeDtypeStruct((count, weight.shape[1]), weight.dtype),
        in_specs=[far()],
        out_specs=vmem(),
        scratch_shapes=[pltpu.SemaphoreType.DMA((LANES,))],
        compiler_params=pltpu.CompilerParams(vmem_limit_bytes=LOADING),
        cost_estimate=cost(0, 4 * count * weight.shape[1]),
        name="load",
    )(weight)


def vmem():
    return pl.BlockSpec(memory_space=pltpu.VMEM)


def far():
    return pl.BlockSpec(memory_space=pltpu.HBM)


def smem():
    return pl.BlockSpec(memory_space=pltpu.SMEM)


def cost(flops, size):
    return pl.CostEstimate(flops=int(flops), bytes_accessed=int(size), transcendentals=0)


def attend_block(scal, queries, sources, new_keys, new_values, group_size):
    length, width = sources[0][0].shape
    rows_in = queries.shape[0]
    groups = width // DH // 2
    rows = rows_in * group_size
    chunk = next(
        length // n
        for n in range(1, length + 1)
        if length % n == 0 and length // n % 128 == 0 and length // n <= MOST_KEYS
    )
    keys = len(sources) * length
    return pl.pallas_call(
        functools.partial(
            attention_kernel,
            sources=len(sources),
            chunk=chunk,
            group_size=group_size,
        ),
        out_shape=jax.ShapeDtypeStruct((groups * rows + STAT_ROWS, DH), jnp.bfloat16),
        in_specs=[smem()] + [vmem()] * 3 + [far()] * (2 * len(sources)),
        out_specs=vmem(),
        scratch_shapes=[
            pltpu.VMEM((groups, rows, DH), jnp.bfloat16),
            pltpu.VMEM((groups, rows, keys), jnp.float32),
            pltpu.VMEM((groups, rows, 128), jnp.float32),
            pltpu.VMEM((groups, rows, 128), jnp.float32),
            pltpu.VMEM((groups, rows, DH), jnp.float32),
            pltpu.VMEM((keys, groups * DH), jnp.bfloat16),
            pltpu.VMEM((keys, groups * DH), jnp.bfloat16),
            pltpu.SemaphoreType.DMA((keys // chunk,)),
            pltpu.SemaphoreType.DMA((keys // chunk,)),
        ],
        compiler_params=pltpu.CompilerParams(vmem_limit_bytes=LARGE),
        cost_estimate=cost(4 * groups * rows * keys * DH * 3, 4 * keys * width),
        name="attend",
    )(scal, queries, new_keys, new_values, *[a for pair in sources for a in pair])


def merged(parts, final, rows_in):
    blocks = (parts[0].shape[0] - STAT_ROWS) // 128
    if final:
        shape = (rows_in, blocks * 128 // rows_in * DH)
    else:
        shape = parts[0].shape
    return pl.pallas_call(
        functools.partial(merge_kernel, final=final, rows_in=rows_in),
        out_shape=jax.ShapeDtypeStruct(shape, jnp.bfloat16),
        in_specs=[vmem()] * len(parts),
        out_specs=vmem(),
        cost_estimate=cost(blocks * 128 * 128 * 8 * len(parts), parts[0].size * 2 * len(parts)),
        compiler_params=pltpu.CompilerParams(vmem_limit_bytes=SMALL),
        name="merge",
    )(*parts)


def project(scal, mine, other, weight, start, count):
    devices = len(mine)
    rows = mine[0].shape[0] * devices
    depth = weight.shape[0]
    return pl.pallas_call(
        functools.partial(projection_kernel, devices=devices, start=start),
        out_shape=jax.ShapeDtypeStruct((rows, count), jnp.bfloat16),
        in_specs=[smem()] + [vmem()] * (2 * devices + 1),
        out_specs=vmem(),
        scratch_shapes=[pltpu.VMEM((rows, depth), jnp.bfloat16)],
        compiler_params=pltpu.CompilerParams(vmem_limit_bytes=MEDIUM),
        cost_estimate=cost(2 * rows * depth * count, 2 * depth * count),
        name="project",
    )(scal, *mine, *other, weight)


def prepare(scal, residual, gain, own, other):
    rows, width = residual.shape
    return pl.pallas_call(
        functools.partial(prepare_kernel, parts=len(own)),
        out_shape=(
            jax.ShapeDtypeStruct((rows, width), jnp.bfloat16),
            jax.ShapeDtypeStruct((2 * rows, 2 * width), jnp.bfloat16),
            jax.ShapeDtypeStruct((8, rows), jnp.float32),
        ),
        in_specs=[smem()] + [vmem()] * (2 + 2 * len(own)),
        out_specs=(vmem(),) * 3,
        cost_estimate=cost(rows * width * 1024, rows * width * 8),
        compiler_params=pltpu.CompilerParams(vmem_limit_bytes=SMALL),
        name="prepare",
    )(scal, residual, gain.reshape(1, width), *own, *other)


def gate_up_part(left, weight, start, count, tile):
    rows2, depth2 = left.shape
    depth = depth2 // 2
    rows = rows2 // 2
    first = start // tile
    out = jax.ShapeDtypeStruct((rows, count), jnp.bfloat16)
    return pl.pallas_call(
        gate_up_kernel,
        grid=(count // tile,),
        out_shape=(out, out),
        in_specs=[
            pl.BlockSpec((rows2, depth2), lambda i: (0, 0)),
            pl.BlockSpec((depth, 2, tile), lambda i: (0, 0, first + i)),
        ],
        out_specs=(
            pl.BlockSpec((rows, tile), lambda i: (0, i)),
            pl.BlockSpec((rows, tile), lambda i: (0, i)),
        ),
        compiler_params=pltpu.CompilerParams(vmem_limit_bytes=LARGE),
        cost_estimate=cost(2 * rows2 * depth2 * count, 4 * depth * count),
        name="gate_up",
    )(left, weight)


def activate(scal, own, other, squares):
    rows, width = own.shape
    return pl.pallas_call(
        activation_kernel,
        out_shape=jax.ShapeDtypeStruct((rows // 2, width), jnp.bfloat16),
        in_specs=[smem()] + [vmem()] * 3,
        out_specs=vmem(),
        cost_estimate=cost(rows * width * 16, rows * width * 5),
        compiler_params=pltpu.CompilerParams(vmem_limit_bytes=SMALL),
        name="activate",
    )(scal, own, other, squares)


def down_project(scal, mine, other, weight, before, last):
    pieces = len(mine)
    half, _ = mine[0].shape
    depth, width = weight.shape
    first = before is None
    inputs = [*mine, *other] + ([] if first else [before])
    scratch = [pltpu.VMEM((2 * half, depth), jnp.bfloat16)]
    if last:
        out_shape = (
            jax.ShapeDtypeStruct((half, width), jnp.float32),
            jax.ShapeDtypeStruct((half, width), jnp.bfloat16),
        )
        out_specs = (vmem(), vmem())
        scratch.append(pltpu.VMEM((2 * half, width), jnp.float32))
    else:
        out_shape = jax.ShapeDtypeStruct((2 * half, width), jnp.float32)
        out_specs = vmem()
    return pl.pallas_call(
        functools.partial(down_kernel, pieces=pieces, first=first, last=last),
        in_specs=[smem()] + [vmem()] * (len(inputs) + 1),
        out_specs=out_specs,
        scratch_shapes=scratch,
        out_shape=out_shape,
        compiler_params=pltpu.CompilerParams(vmem_limit_bytes=MEDIUM),
        cost_estimate=cost(4 * half * depth * width, 2 * depth * width),
        name="down",
    )(scal, *inputs, weight)


def fold_kernel(scal_ref, own_ref, come_ref, away_ref, keep_ref):
    upper = scal_ref[0]
    width = keep_ref.shape[1]
    for out_ref, which in ((away_ref, 1 - upper), (keep_ref, upper)):
        span = pl.ds(pl.multiple_of(which * width, 128), width)
        out_ref[...] = (
            own_ref[:, span].astype(jnp.float32) + come_ref[:, span].astype(jnp.float32)
        ).astype(jnp.bfloat16)


def fold(scal, own, come):
    rows, width = own.shape
    out = jax.ShapeDtypeStruct((rows, width // 2), jnp.bfloat16)
    return pl.pallas_call(
        fold_kernel,
        out_shape=(out, out),
        in_specs=[smem()] + [vmem()] * 2,
        out_specs=(vmem(), vmem()),
        compiler_params=pltpu.CompilerParams(vmem_limit_bytes=SMALL),
        cost_estimate=cost(rows * width, rows * width * 6),
        name="fold",
    )(scal, own, come)


def half_of(value, which, axis=1):
    size = value.shape[axis] // 2
    return lax.dynamic_slice_in_dim(value, which * size, size, axis)


def spread(value, bits):
    pieces = {0: value}
    for bit in reversed(bits):
        for mask in list(pieces):
            pieces[mask | bit] = exchanged(pieces[mask], "ctx", bit)
    return [pieces[mask] for mask in range(len(pieces))]


def on_device_line(
    queries,
    cache_keys,
    cache_values,
    new_keys,
    new_values,
    cache_blocks,
    residual,
    norm_gain,
    out_weight,
    gate_up,
    down_weight,
):
    devices = lax.axis_size("ctx")
    place = lax.axis_index("ctx")
    core = lax.axis_index("khalf")
    side = lax.axis_index("kv")
    group_size = HQ // KVH
    rows_in = queries.shape[0]
    length = cache_keys.shape[0]
    mine_valid, other_valid = (
        jnp.clip(cache_blocks[0] * BLOCK - (place * 2 + c) * length, 0, length)
        for c in (core, 1 - core)
    )
    bits = [1 << b for b in range(devices.bit_length() - 1)]
    sources = [place ^ mask for mask in range(devices)]
    blocks = [
        sum((source // bit) % 2 * (devices // (2 * bit)) for bit in bits) for source in sources
    ]
    groups = cache_keys.shape[1] // DH // 2
    offsets = [(source - place) * rows_in for source in sources]

    def packed(*values):
        return jnp.stack(values).astype(jnp.int32)

    early = (
        half_of(queries, core),
        half_of(new_keys, core),
        half_of(new_values, core),
        [packed(mine_valid, other_valid, o, core * groups) for o in offsets],
        packed(core, *((place - s) % devices for s in range(devices))),
        packed(core, side),
        packed(core, side, *blocks),
        [packed((place // bit) % 2) for bit in bits],
    )
    early = lax.optimization_barrier(early)
    q_mine, fresh_keys, fresh_values, visit_scals, source_scal, core_scal, down_scal, bit_scals = early
    k_there = exchanged(cache_keys, "khalf", 1)
    v_there = exchanged(cache_values, "khalf", 1)
    visiting = spread(q_mine, bits)
    k_here = loaded(cache_keys, 0, length)
    v_here = loaded(cache_values, 0, length)
    here, there = (k_here, v_here), (k_there, v_there)
    parts = []
    last = None
    for mask in [*range(1, devices), 0]:
        visitor = visiting[mask]
        if last is not None:
            visitor, last = lax.optimization_barrier((visitor, last))
        last = attend_block(
            visit_scals[mask], visitor, [here, there], fresh_keys, fresh_values, group_size
        )
        parts.append(exchanged(last, "ctx", mask) if mask else last)
    attention = merged(parts, True, rows_in)
    mine = []
    for s in range(devices):
        mine.append(rotated(attention, "ctx", s) if s else attention)
    other = [exchanged(a, "khalf", 1) for a in mine]
    out_near = loaded(out_weight, 0, out_weight.shape[0])
    own, come = [], []
    width = out_weight.shape[1] // SLABS
    for slab in range(SLABS):
        own.append(project(source_scal, mine, other, out_near, slab * width, width))
        come.append(exchanged(own[-1], "kv", 1))
    hidden, left, squares = prepare(core_scal, residual, norm_gain, own, come)
    for bit in bits:
        squares = squares + exchanged(squares, "ctx", bit)
    squares = squares + exchanged(squares, "khalf", 1)
    unit = gate_up.shape[2] // sum(STREAMS)
    starts = [unit * sum(STREAMS[:i]) for i in range(len(STREAMS))]
    spans = [unit * share for share in STREAMS]
    down = None
    down_near = []
    for start, span in zip(starts, spans):
        down_near.append(loaded(down_weight, start, span))
    for stream, (start, span) in enumerate(zip(starts, spans)):
        keep, send = gate_up_part(left, gate_up, start, span, unit)
        come = exchanged(send, "khalf", 1)
        for bit, bit_scal in zip(bits, bit_scals):
            away, keep = fold(bit_scal, keep, come)
            if bit == 1:
                away, left = lax.optimization_barrier((away, left))
            come = exchanged(away, "ctx", bit)
        activated = activate(core_scal, keep, come, squares)
        mine = spread(activated, bits)
        other = [exchanged(piece, "khalf", 1) for piece in mine]
        down = down_project(
            down_scal, mine, other, down_near[stream], down, stream == len(STREAMS) - 1
        )
    keep, send = down
    come = exchanged(send, "kv", 1)
    kept = half_of(hidden, side, 0)
    return (kept.astype(jnp.float32) + keep + come.astype(jnp.float32)).astype(jnp.bfloat16)


def line_fits(mesh, keys_shape, hidden_width):
    sizes = dict(mesh.shape)
    ctx, kv, khalf = sizes["ctx"], sizes["kv"], sizes["khalf"]
    groups = keys_shape[1] // kv // DH
    length = keys_shape[0] // (sizes["groups"] * ctx * khalf)
    return (
        ctx & (ctx - 1) == 0
        and kv == 2
        and khalf == 2
        and groups % 2 == 0
        and length % 128 == 0
        and hidden_width // kv % (sum(STREAMS) * ctx * 128) == 0
    )


def solution(mesh):
    def on_device(*arguments):
        keys, gate_up = arguments[1], arguments[9]
        sizes = dict(mesh.shape)
        keys_shape = (
            keys.shape[0] * sizes["groups"] * sizes["ctx"] * sizes["khalf"],
            keys.shape[1] * sizes["kv"],
        )
        if line_fits(mesh, keys_shape, gate_up.shape[2] * sizes["kv"]):
            return on_device_line(*arguments)
        return on_device_any(*arguments)

    in_specs = (
        P(("groups", "ctx"), "kv"),
        P(("groups", "ctx", "khalf"), "kv"),
        P(("groups", "ctx", "khalf"), "kv"),
        P(("groups", "ctx"), "kv"),
        P(("groups", "ctx"), "kv"),
        P("groups"),
        P("groups", ("ctx", "khalf")),
        P(("ctx", "khalf")),
        P("kv", ("ctx", "khalf")),
        P(("ctx", "khalf"), None, "kv"),
        P("kv", ("ctx", "khalf")),
    )
    out_specs = P(("groups", "kv"), ("ctx", "khalf"))
    return jax.shard_map(
        on_device, mesh=mesh, in_specs=in_specs, out_specs=out_specs, check_vma=False
    )
```
